256 devices in a mesh: blk: 32 (over y_lo, z, core), frq: 8 (over y_hi, x).
Axes of the slice: x: 4, y: 4 (y_hi: 2, y_lo: 2; y = y_hi * 2 + y_lo), z: 8, core: 2. Of those that a mesh axis runs over, the one named last changes fastest.
Arguments:
- spectra: bfloat16 [2, 8192, 4, 2048], P(None, 'blk', None, 'frq'), may hold values from -6 to 6
- channel_valid: int32 [8192], P('blk'), may hold values 0 or 1
Outputs:
- stacked: float32 [32, 4, 201, 256], P('blk', None, None, 'frq')
The draws below stay inside these ranges and needn't reach their ends.
Inputs may be any that keep to these rules, and one draw needn't show every extreme that they name: `channel_valid`: 1 marks a usable channel.
All inputs are finite; a program needn't handle non-finite values. No bound on the sum of `channel_valid` on one device may be relied on, other than what follows from the above.
Results may differ from the reference program's by a relative error of at most 0.006.
Values may be sent and summed in bfloat16 or wider, within the bound.
A program may use at most 128 MiB of HBM per device.

```python
import math
import jax
import jax.numpy as jnp
from jax import lax

CB = 256
W = 4
F = 2048
LAGS = 201
ROUNDS = 4
CH = 8192
N_BLK = 32


def with_ends(array, key, smallest, top_value):
    place = [jax.random.randint(jax.random.fold_in(key, axis), (), 0, length) for axis, length in enumerate(array.shape)]
    main_axis = array.shape.index(max(array.shape))
    beside = place[:main_axis] + [(place[main_axis] + 1) % array.shape[main_axis]] + place[main_axis + 1:]
    return array.at[tuple(place)].set(smallest).at[tuple(beside)].set(top_value)


def shard_levels(key, shape, split, smallest, top_value):
    level, own = 1.0, jax.random.fold_in(key, 6)
    for dim, blocks in split:
        heights = jnp.exp(jax.random.uniform(jax.random.fold_in(own, dim), (blocks,), jnp.float32, smallest / len(split), top_value / len(split)))
        level = level * jnp.repeat(heights, shape[dim] // blocks).reshape([-1 if axis == dim else 1 for axis in range(len(shape))])
    return level


def noise(key, extent, deviation, reach, split=(), held_as=jnp.bfloat16):
    gain = shard_levels(key, extent, split, -0.22, 0.18) if split else 1.0
    result = jax.random.normal(key, extent, jnp.float32) * deviation * gain
    return jnp.minimum(jnp.maximum(result, -reach), reach).astype(held_as)


def setup_inputs(seed: int = 0) -> dict:
    key_of = jax.random.split(jax.random.key(seed), 3)
    spectra = noise(key_of[0], (2, CH, W, F), 1.0, 6.0, ((1, 32), (3, 8)))
    channel_valid = with_ends((jax.random.randint(key_of[1], (CH,), 0, 8) < 7).astype(jnp.int32), jax.random.fold_in(key_of[1], 1), 0, 1)
    return {"spectra": spectra, "channel_valid": channel_valid}


def matmul_high(left, right):
    return jnp.dot(left, right, precision=lax.Precision.HIGHEST, preferred_element_type=jnp.float32)

def angle_table(first_index, second_index, period):
    product = jnp.mod(first_index[:, None] * second_index[None, :], period)
    return 2.0 * math.pi / period * product.astype(jnp.float32)

def split_table(table):
    upper = table.astype(jnp.bfloat16)
    lower = (table - upper.astype(jnp.float32)).astype(jnp.bfloat16)
    return (upper, lower)

def twiddle_product(pair, data):
    return jnp.dot(pair[0], data, preferred_element_type=jnp.float32) + jnp.dot(pair[1], data, preferred_element_type=jnp.float32)

def to_wavenumber(spectrum_in, cos_pair, sin_pair):
    channels = spectrum_in.shape[1]
    flattened = spectrum_in.reshape(2, channels, -1)
    real_part = twiddle_product(cos_pair, flattened[0]) + twiddle_product(sin_pair, flattened[1])
    imag_part = twiddle_product(cos_pair, flattened[1]) - twiddle_product(sin_pair, flattened[0])
    return jnp.stack([real_part, imag_part])

def lag_terms(own_hat, far_hat, windows, inv_cos, inv_sin, lag_cos, lag_sin, normalizer):
    length = own_hat.shape[1]
    own_hat = own_hat.reshape(2, length, windows, -1)
    far_hat = far_hat.reshape(2, length, windows, -1)
    cross_real = lax.optimization_barrier(jnp.sum(own_hat[0] * far_hat[0] + own_hat[1] * far_hat[1], axis=1))
    cross_imag = lax.optimization_barrier(jnp.sum(own_hat[1] * far_hat[0] - own_hat[0] * far_hat[1], axis=1))
    stack_real = matmul_high(inv_cos, cross_real) - matmul_high(inv_sin, cross_imag)
    stack_imag = matmul_high(inv_sin, cross_real) + matmul_high(inv_cos, cross_imag)
    return normalizer * (matmul_high(lag_cos, stack_real.T) - matmul_high(lag_sin, stack_imag.T))

def reference(spectra, channel_valid):
    spectra_f = spectra.astype(jnp.float32)
    mean_power = lax.optimization_barrier(jnp.mean(spectra_f[0] * spectra_f[0] + spectra_f[1] * spectra_f[1], axis=1, keepdims=True))
    whiten_scale = channel_valid.astype(jnp.float32)[:, None, None] / jnp.maximum(jnp.sqrt(mean_power), 0.5)
    whitened = (spectra_f * whiten_scale[None]).astype(jnp.bfloat16)
    blocks = jnp.moveaxis(whitened.reshape(2, N_BLK, CB, W, F), 1, 0)
    length = 2 * CB
    chan_index = jnp.arange(CB, dtype=jnp.int32)
    wave_index = jnp.arange(length, dtype=jnp.int32)
    fwd_angle = angle_table(wave_index, chan_index, length)
    cos_pair = split_table(jnp.cos(fwd_angle))
    sin_pair = split_table(jnp.sin(fwd_angle))
    inv_angle = angle_table(chan_index - CB // 2, wave_index, length)
    inv_cos, inv_sin = (jnp.cos(inv_angle) / length, jnp.sin(inv_angle) / length)
    lag_index = jnp.arange(LAGS, dtype=jnp.int32) - (LAGS - 1) // 2
    freq_index = jnp.arange(F, dtype=jnp.int32)
    lag_angle = angle_table(lag_index, freq_index, 2 * F)
    lag_cos, lag_sin = (jnp.cos(lag_angle), jnp.sin(lag_angle))
    normalizer = 1.0 / math.sqrt(W * CB * F)

    def scan_block(history, block):
        own_hat = to_wavenumber(block, cos_pair, sin_pair)
        results = [lag_terms(own_hat, history[index], W, inv_cos, inv_sin, lag_cos, lag_sin, normalizer) for index in range(ROUNDS)]
        history = jnp.concatenate([own_hat[None], history[:-1]], axis=0)
        return (history, jnp.stack(results))
    start_history = jnp.zeros((ROUNDS, 2, length, W * F), jnp.float32)
    final_history, stacked = lax.scan(scan_block, start_history, blocks)
    return stacked
```

```python
import functools
import math

import jax
import jax.numpy as jnp
import ml_dtypes
import numpy as np
from jax import lax
from jax.experimental import pallas as pl
from jax.experimental.pallas import tpu as pltpu
from jax.sharding import PartitionSpec as P

LAGS = 201
ROUNDS = 4
CB = 256
W = 4
M = 384
K = 128
TAU = 256
MESH = pl.DeviceIdType.MESH
PAIRS = 8


def forward_table():
    angle = 2.0 * np.pi / M * (np.outer(np.arange(M), np.arange(CB)) % M)
    cos, sin = np.cos(angle), np.sin(angle)
    return np.block([[cos, sin], [-sin, cos]]).astype(ml_dtypes.bfloat16)


def inverse_table(scale):
    angle = 2.0 * np.pi / M * (np.outer(np.arange(CB) - CB // 2, np.arange(M)) % M)
    cos, sin = scale * np.cos(angle), scale * np.sin(angle)
    return np.block([[cos, -sin], [sin, cos]]).astype(ml_dtypes.bfloat16)


def lag_table(freq_total):
    lag = np.arange(TAU) - (LAGS - 1) // 2
    angle = np.pi / freq_total * (np.outer(np.arange(freq_total), lag) % (2 * freq_total))
    keep = np.arange(TAU) < LAGS
    cos = np.where(keep, np.cos(angle), 0.0).reshape(-1, K, TAU)
    sin = np.where(keep, np.sin(angle), 0.0).reshape(-1, K, TAU)
    return np.concatenate([cos, -sin], axis=1).astype(ml_dtypes.bfloat16)


PAIR_LIST = (
    ((0, 0), (1, 1)),
    ((0, 0), (1, 0)),
    ((2, 0), (1, 1)),
    ((2, 0), (1, 0)),
    ((0, 1), (0, 0)),
    ((0, 1), (1, 1)),
    ((0, 1), (1, 0)),
    ((2, 1), (1, 1)),
)


def kernel(
    n_blk, n_frq, x_ref, fwd_hbm, inv_hbm, lag_hbm, out_ref,
    fwd, inv, lag, near, hats, acc, part_out, part_in, piece_out, piece_in,
    table_sem, local_sem, send_sem, recv_sem, part_send, part_recv, piece_send, piece_recv,
):
    blk = lax.axis_index("blk")
    frq = lax.axis_index("frq")
    chips = n_blk // 2
    rows = CB // n_frq
    chip, core = blk // 2, blk % 2
    right = (chip + 1) % chips
    left = (chip + chips - 1) % chips

    barrier = pltpu.get_barrier_semaphore()
    peers = [(chip * 2 + 1 - core, frq)]
    for c in range(2):
        peers += [(right * 2 + c, frq), (left * 2 + c, frq)]
    for off in range(1, n_frq):
        other = (frq + off) % n_frq
        peers += [(blk, other), (right * 2 + core, other), (left * 2 + core, other)]
    for peer in peers:
        pl.semaphore_signal(barrier, inc=1, device_id=peer, device_id_type=MESH)

    tables = [
        pltpu.make_async_copy(fwd_hbm, fwd, table_sem.at[0]),
        pltpu.make_async_copy(inv_hbm, inv, table_sem.at[1]),
        pltpu.make_async_copy(lag_hbm.at[frq * 2 + core], lag, table_sem.at[2]),
    ]
    for copy in tables:
        copy.start()
    acc[...] = jnp.zeros_like(acc)
    pl.semaphore_wait(barrier, len(peers))

    def local_copy(w):
        return pltpu.make_async_copy(x_ref.at[core, w], near.at[0, w, core], local_sem.at[w])

    def partner_copy(w):
        return pltpu.make_async_remote_copy(
            src_ref=x_ref.at[1 - core, w],
            dst_ref=near.at[0, w, core],
            send_sem=send_sem.at[0, w, 0],
            recv_sem=recv_sem.at[0, w, core],
            device_id=(chip * 2 + 1 - core, frq),
            device_id_type=MESH,
        )

    def chip_copy(slot, w, half):
        return pltpu.make_async_remote_copy(
            src_ref=x_ref.at[half, w],
            dst_ref=near.at[slot, w, core],
            send_sem=send_sem.at[slot, w, half],
            recv_sem=recv_sem.at[slot, w, core],
            device_id=((right if slot == 1 else left) * 2 + half, frq),
            device_id_type=MESH,
        )

    for w in range(W):
        local_copy(w).start()
        for half in range(2):
            chip_copy(1, w, half).start()
            chip_copy(2, w, half).start()
        partner_copy(w).start()
    for copy in tables:
        copy.wait()

    def wait_landed(slot, w, c):
        pltpu.make_async_copy(near.at[slot, w, c], near.at[slot, w, c], recv_sem.at[slot, w, c]).wait()

    def hat(slot, w):
        data = jnp.concatenate([near[slot, w, 0], near[slot, w, 1]], axis=1)
        hats[slot] = jnp.dot(fwd[...], data, preferred_element_type=jnp.float32)

    def window(w, carry):
        local_copy(w).wait()
        wait_landed(0, w, 1 - core)
        hat(0, w)
        for slot in (1, 2):
            for c in range(2):
                wait_landed(slot, w, c)
            hat(slot, w)

        def tile(t, inner):
            re = pl.ds(pl.multiple_of(t * 8, 8), 8)
            im = pl.ds(pl.multiple_of(M + t * 8, 8), 8)
            value = {}
            for slot in range(3):
                for c in range(2):
                    lanes = slice(c * K, (c + 1) * K)
                    value[slot, c] = (hats[slot, re, lanes], hats[slot, im, lanes])
            for index, (one, two) in enumerate(PAIR_LIST):
                (ar, ai), (br, bi) = value[one], value[two]
                acc[index, re] += ar * br + ai * bi
                acc[index, im] += ai * br - ar * bi
            return inner

        return lax.fori_loop(0, M // 8, tile, carry)

    lax.fori_loop(0, W, window, 0)

    def correlations(index):
        both = jnp.concatenate([acc[index], acc[index + 1]], axis=1).astype(jnp.bfloat16)
        stack = jnp.dot(inv[...], both, preferred_element_type=jnp.float32).astype(jnp.bfloat16)
        for c in range(2):
            lanes = slice(c * K, (c + 1) * K)
            pair = jnp.concatenate([stack[:CB, lanes], stack[CB:, lanes]], axis=1)
            yield jnp.dot(pair, lag[...], preferred_element_type=jnp.float32)

    def part_copy(j):
        return pltpu.make_async_remote_copy(
            src_ref=part_out.at[j],
            dst_ref=part_in.at[j],
            send_sem=part_send.at[j],
            recv_sem=part_recv.at[j],
            device_id=(chip * 2 + 1 - core, frq),
            device_id_type=MESH,
        )

    for j in range(0, ROUNDS, 2):
        for c, value in enumerate(correlations((1 - core) * ROUNDS + j)):
            part_out[j + c] = value.astype(jnp.bfloat16)
            part_copy(j + c).start()

    def owner(j):
        shift = (0, 0, 1 - core, 1)[j]
        return ((chip + shift) % chips) * 2 + core

    def piece_copy(j, off):
        other = (frq + off) % n_frq
        return pltpu.make_async_remote_copy(
            src_ref=piece_out.at[j, pl.ds(pl.multiple_of(other * rows, rows), rows)],
            dst_ref=piece_in.at[j, frq],
            send_sem=piece_send.at[j, off],
            recv_sem=piece_recv.at[j, frq],
            device_id=(owner(j), other),
            device_id_type=MESH,
        )

    def own_copy(j):
        return pltpu.make_async_copy(
            piece_out.at[j, pl.ds(pl.multiple_of(frq * rows, rows), rows)],
            piece_in.at[j, frq],
            piece_recv.at[j, frq],
        )

    for j in range(0, ROUNDS, 2):
        for c, value in enumerate(correlations(core * ROUNDS + j)):
            part_copy(j + c).wait_recv()
            piece_out[j + c] = (value + part_in[j + c].astype(jnp.float32)).astype(jnp.bfloat16)
            for off in range(1, n_frq):
                piece_copy(j + c, off).start()
            if j + c < 2:
                own_copy(j + c).start()
            elif j + c == 3:
                piece_copy(j + c, 0).start()
            else:
                @pl.when(core == 0)
                def _():
                    piece_copy(2, 0).start()

                @pl.when(core == 1)
                def _():
                    own_copy(2).start()

    for j in range(ROUNDS):
        total = jnp.zeros((rows, TAU), jnp.float32)
        for f in range(n_frq):
            pltpu.make_async_copy(piece_in.at[j, f], piece_in.at[j, f], piece_recv.at[j, f]).wait()
            total += piece_in[j, f].astype(jnp.float32)
        total = jnp.where(blk > j, total, 0.0)
        out_ref[j] = total[:, :LAGS]

    for w in range(W):
        partner_copy(w).wait_send()
        for half in range(2):
            chip_copy(1, w, half).wait_send()
            chip_copy(2, w, half).wait_send()
    for j in range(ROUNDS):
        part_copy(j).wait_send()
        for off in range(1, n_frq):
            piece_copy(j, off).wait_send()
    piece_copy(3, 0).wait_send()

    @pl.when(core == 0)
    def _():
        piece_copy(2, 0).wait_send()


def on_device(n_blk, n_frq, spectra, channel_valid):
    freq_local = spectra.shape[3]
    freq_total = freq_local * n_frq
    spectra_f = spectra.astype(jnp.float32)
    mean_power = jnp.mean(
        spectra_f[0] * spectra_f[0] + spectra_f[1] * spectra_f[1], axis=1, keepdims=True
    )
    whiten_scale = channel_valid.astype(jnp.float32)[:, None, None] / jnp.maximum(
        jnp.sqrt(mean_power), 0.5
    )
    whitened = (spectra_f * whiten_scale[None]).astype(jnp.bfloat16)
    halves = whitened.reshape(2, CB, W, 2, K).transpose(3, 2, 0, 1, 4).reshape(2, W, 2 * CB, K)
    rows = CB // n_frq
    scale = 1.0 / (M * math.sqrt(W * CB * freq_total))
    vmem = pl.BlockSpec(memory_space=pltpu.VMEM)
    hbm = pl.BlockSpec(memory_space=pl.ANY)
    dma = pltpu.SemaphoreType.DMA
    stacked = pl.pallas_call(
        functools.partial(kernel, n_blk, n_frq),
        out_shape=jax.ShapeDtypeStruct((ROUNDS, rows, LAGS), jnp.float32),
        in_specs=[vmem, hbm, hbm, hbm],
        out_specs=vmem,
        scratch_shapes=[
            pltpu.VMEM((2 * M, 2 * CB), jnp.bfloat16),
            pltpu.VMEM((2 * CB, 2 * M), jnp.bfloat16),
            pltpu.VMEM((2 * K, TAU), jnp.bfloat16),
            pltpu.VMEM((3, W, 2, 2 * CB, K), jnp.bfloat16),
            pltpu.VMEM((3, 2 * M, 2 * K), jnp.float32),
            pltpu.VMEM((PAIRS, 2 * M, K), jnp.float32),
            pltpu.VMEM((ROUNDS, CB, TAU), jnp.bfloat16),
            pltpu.VMEM((ROUNDS, CB, TAU), jnp.bfloat16),
            pltpu.VMEM((ROUNDS, CB, TAU), jnp.bfloat16),
            pltpu.VMEM((ROUNDS, n_frq, rows, TAU), jnp.bfloat16),
            dma((3,)),
            dma((W,)),
            dma((3, W, 2)),
            dma((3, W, 2)),
            dma((ROUNDS,)),
            dma((ROUNDS,)),
            dma((ROUNDS, n_frq)),
            dma((ROUNDS, n_frq)),
        ],
        compiler_params=pltpu.CompilerParams(collective_id=0, has_side_effects=True),
    )(
        halves,
        jnp.asarray(forward_table()),
        jnp.asarray(inverse_table(scale)),
        jnp.asarray(lag_table(freq_total)),
    )
    return stacked.transpose(0, 2, 1)[None]


def solution(mesh):
    return jax.shard_map(
        functools.partial(on_device, mesh.shape["blk"], mesh.shape["frq"]),
        mesh=mesh,
        in_specs=(P(None, "blk", None, "frq"), P("blk")),
        out_specs=P("blk", None, None, "frq"),
        check_vma=False,
    )
```

```python
import functools
import math

import jax
import jax.numpy as jnp
import ml_dtypes
import numpy as np
from jax import lax
from jax.experimental import pallas as pl
from jax.experimental.pallas import tpu as pltpu
from jax.sharding import PartitionSpec as P

LAGS = 201
ROUNDS = 4
CB = 256
W = 4
M = 384
K = 128
TAU = 256
EARLY = 3
MESH = pl.DeviceIdType.MESH


def forward_table():
    angle = 2.0 * np.pi / M * (np.outer(np.arange(M), np.arange(CB)) % M)
    cos, sin = np.cos(angle), np.sin(angle)
    return np.block([[cos, sin], [-sin, cos]]).astype(ml_dtypes.bfloat16)


def inverse_table(scale):
    angle = 2.0 * np.pi / M * (np.outer(np.arange(CB) - CB // 2, np.arange(M)) % M)
    cos, sin = scale * np.cos(angle), scale * np.sin(angle)
    return np.block([[cos, -sin], [sin, cos]]).astype(ml_dtypes.bfloat16)


def lag_tables(freq_total):
    lag = np.arange(TAU) - (LAGS - 1) // 2
    keep = np.arange(TAU) < LAGS

    def waves(freq):
        angle = np.pi / freq_total * (np.outer(freq, lag) % (2 * freq_total))
        return np.stack([np.where(keep, np.cos(angle), 0.0), np.where(keep, np.sin(angle), 0.0)])

    fine = waves(np.arange(K)).astype(np.float32)
    coarse = waves(np.arange(0, freq_total, K)).transpose(1, 0, 2).astype(np.float32)
    return fine, coarse


C, D, B, E, A, F = (0, 0), (0, 1), (1, 0), (1, 1), (2, 0), (2, 1)
PHASE_PAIRS = (
    ((C, B), (E, B), (D, C), (D, B)),
    ((C, A), (E, A), (D, A), (F, B)),
)


def kernel(
    n_blk, n_frq, raw_hbm, valid_ref, fwd_hbm, inv_hbm, fine_hbm, coarse_hbm, out_ref,
    raw, fwd, inv, fine, coarse, lag, column, mine, near, hats, acc, part_out, part_in, piece_out, piece_in,
    load_sem, local_sem, send_sem, recv_sem, part_send, part_recv, piece_send, piece_recv,
):
    blk = lax.axis_index("blk")
    frq = lax.axis_index("frq")
    chips = n_blk // 2
    rows = CB // n_frq
    chip, core = blk // 2, blk % 2
    right = (chip + 1) % chips
    left = (chip + chips - 1) % chips
    partner = (chip * 2 + 1 - core, frq)

    loads = [
        pltpu.make_async_copy(raw_hbm, raw, load_sem.at[0]),
        pltpu.make_async_copy(fwd_hbm, fwd, load_sem.at[1]),
        pltpu.make_async_copy(inv_hbm, inv, load_sem.at[2]),
        pltpu.make_async_copy(fine_hbm, fine, load_sem.at[3]),
        pltpu.make_async_copy(coarse_hbm.at[frq * 2 + core], coarse, load_sem.at[4]),
    ]
    for copy in loads:
        copy.start()

    barrier = pltpu.get_barrier_semaphore()
    peers = [partner]
    for c in range(2):
        peers += [(right * 2 + c, frq), (left * 2 + c, frq)]
    for off in range(1, n_frq):
        other = (frq + off) % n_frq
        peers += [(blk, other), (right * 2 + core, other), (left * 2 + core, other)]
    for peer in peers:
        pl.semaphore_signal(barrier, inc=1, device_id=peer, device_id_type=MESH)

    here = lax.broadcasted_iota(jnp.int32, (K, K), 0) == lax.broadcasted_iota(jnp.int32, (K, K), 1)
    for part in range(CB // K):
        row = valid_ref[part : part + 1, :].astype(jnp.float32)
        spread = jnp.where(here, jnp.broadcast_to(row, (K, K)), 0.0)
        total = jnp.sum(spread, axis=1, keepdims=True)
        column[part * K : (part + 1) * K] = jnp.broadcast_to(total, (K, K))

    loads[0].wait()

    def whiten(t, carry):
        real = pl.ds(pl.multiple_of(t * 16, 16), 16)
        imag = pl.ds(pl.multiple_of(CB + t * 16, 16), 16)
        keep = column[real]
        for half in range(2):
            values = [
                (raw[half, w, real].astype(jnp.float32), raw[half, w, imag].astype(jnp.float32))
                for w in range(W)
            ]
            power = sum(re * re + im * im for re, im in values) * (1.0 / W)
            factor = keep / jnp.maximum(jnp.sqrt(power), 0.5)
            for w, (re, im) in enumerate(values):
                mine[half, w, real] = (re * factor).astype(jnp.bfloat16)
                mine[half, w, imag] = (im * factor).astype(jnp.bfloat16)
        return carry

    lax.fori_loop(0, CB // 16, whiten, 0, unroll=2)
    pl.semaphore_wait(barrier, len(peers))

    def local_copy(w):
        return pltpu.make_async_copy(mine.at[core, w], near.at[0, w, core], local_sem.at[w])

    def partner_copy(w):
        return pltpu.make_async_remote_copy(
            src_ref=mine.at[1 - core, w],
            dst_ref=near.at[0, w, core],
            send_sem=send_sem.at[0, w, 0],
            recv_sem=recv_sem.at[0, w, core],
            device_id=partner,
            device_id_type=MESH,
        )

    def chip_copy(phase, w, half):
        rightward = core == (1 if phase == 1 else 0)
        side = 1 - core if phase == 1 else core
        return pltpu.make_async_remote_copy(
            src_ref=mine.at[half, w],
            dst_ref=near.at[phase, w, side],
            send_sem=send_sem.at[phase, w, half],
            recv_sem=recv_sem.at[phase, w, side],
            device_id=(jnp.where(rightward, right, left) * 2 + half, frq),
            device_id_type=MESH,
        )

    for w in range(W):
        for half in range(2):
            chip_copy(1, w, half).start()
        partner_copy(w).start()
        local_copy(w).start()

    acc[...] = jnp.zeros_like(acc)
    for copy in loads[1:]:
        copy.wait()
    fine_cos, fine_sin = fine[0], fine[1]
    coarse_cos, coarse_sin = coarse[0:1], coarse[1:2]
    lag[:K] = (fine_cos * coarse_cos - fine_sin * coarse_sin).astype(jnp.bfloat16)
    lag[K:] = (-(fine_sin * coarse_cos + fine_cos * coarse_sin)).astype(jnp.bfloat16)

    def wait_landed(slot, w, c):
        pltpu.make_async_copy(near.at[slot, w, c], near.at[slot, w, c], recv_sem.at[slot, w, c]).wait()

    def hat(slot, w):
        data = jnp.concatenate([near[slot, w, 0], near[slot, w, 1]], axis=1)
        hats[slot, w] = jnp.dot(fwd[...], data, preferred_element_type=jnp.float32)

    def cross(phase, w):
        pairs = PHASE_PAIRS[phase - 1]
        used = sorted({block for pair in pairs for block in pair})

        def tile(t, carry):
            re = pl.ds(pl.multiple_of(t * 8, 8), 8)
            im = pl.ds(pl.multiple_of(M + t * 8, 8), 8)
            value = {}
            for slot, c in used:
                lanes = slice(c * K, (c + 1) * K)
                value[slot, c] = (hats[slot, w, re, lanes], hats[slot, w, im, lanes])
            for index, (one, two) in enumerate(pairs):
                (ar, ai), (br, bi) = value[one], value[two]
                acc[phase - 1, index, re] += ar * br + ai * bi
                acc[phase - 1, index, im] += ai * br - ar * bi
            return carry

        lax.fori_loop(0, M // 8, tile, 0, unroll=2)

    def correlations(phase, index):
        both = jnp.concatenate([acc[phase - 1, index], acc[phase - 1, index + 1]], axis=1)
        stack = jnp.dot(inv[...], both.astype(jnp.bfloat16), preferred_element_type=jnp.float32)
        stack = stack.astype(jnp.bfloat16)
        for c in range(2):
            lanes = slice(c * K, (c + 1) * K)
            pair = jnp.concatenate([stack[:CB, lanes], stack[CB:, lanes]], axis=1)
            yield jnp.dot(pair, lag[...], preferred_element_type=jnp.float32)

    def part_copy(phase, i):
        return pltpu.make_async_remote_copy(
            src_ref=part_out.at[phase - 1, i],
            dst_ref=part_in.at[phase - 1, i],
            send_sem=part_send.at[phase - 1, i],
            recv_sem=part_recv.at[phase - 1, i],
            device_id=partner,
            device_id_type=MESH,
        )

    def place(phase, i):
        if phase == 1:
            return (0, 0) if i == 0 else (2 - core, 1 - core)
        return (1 + core, 0) if i == 0 else (3, 1)

    def piece_rows(other):
        return pl.ds(pl.multiple_of(other * rows, rows), rows)

    def piece_copy(phase, i, off):
        j, shift = place(phase, i)
        other = (frq + off) % n_frq
        return pltpu.make_async_remote_copy(
            src_ref=piece_out.at[phase - 1, i, piece_rows(other)],
            dst_ref=piece_in.at[j, frq],
            send_sem=piece_send.at[phase - 1, i, off],
            recv_sem=piece_recv.at[j, frq],
            device_id=((chip + shift) % chips * 2 + core, other),
            device_id_type=MESH,
        )

    def own_copy(phase, i):
        j, _ = place(phase, i)
        return pltpu.make_async_copy(
            piece_out.at[phase - 1, i, piece_rows(frq)], piece_in.at[j, frq], piece_recv.at[j, frq]
        )

    def scatter(phase):
        for i, value in enumerate(correlations(phase, (1 - core) * 2)):
            part_out[phase - 1, i] = value.astype(jnp.bfloat16)
            part_copy(phase, i).start()
        for i, value in enumerate(correlations(phase, core * 2)):
            part_copy(phase, i).wait_recv()
            both = value + part_in[phase - 1, i].astype(jnp.float32)
            piece_out[phase - 1, i] = both.astype(jnp.bfloat16)
            for off in range(1, n_frq):
                piece_copy(phase, i, off).start()
            if i == 0:
                own_copy(phase, i).start()
            elif phase == 2:
                piece_copy(phase, i, 0).start()
            else:
                @pl.when(core == 0)
                def _():
                    piece_copy(1, 1, 0).start()

                @pl.when(core == 1)
                def _():
                    own_copy(1, 1).start()

    def first(w, carry):
        local_copy(w).wait()
        wait_landed(0, w, 1 - core)
        hat(0, w)
        for c in range(2):
            wait_landed(1, w, c)
        hat(1, w)
        cross(1, w)
        return carry

    lax.fori_loop(0, EARLY, first, 0)
    for w in range(W):
        for half in range(2):
            chip_copy(2, w, half).start()
    lax.fori_loop(EARLY, W, first, 0)
    scatter(1)

    def second(w, carry):
        for c in range(2):
            wait_landed(2, w, c)
        hat(2, w)
        cross(2, w)
        return carry

    lax.fori_loop(0, W, second, 0)
    scatter(2)

    for j in range(ROUNDS):
        total = jnp.zeros((rows, TAU), jnp.float32)
        for f in range(n_frq):
            pltpu.make_async_copy(piece_in.at[j, f], piece_in.at[j, f], piece_recv.at[j, f]).wait()
            total += piece_in[j, f].astype(jnp.float32)
        total = jnp.where(blk > j, total, 0.0)
        out_ref[j] = total[:, :LAGS]

    for w in range(W):
        partner_copy(w).wait_send()
        for half in range(2):
            chip_copy(1, w, half).wait_send()
            chip_copy(2, w, half).wait_send()
    for phase in (1, 2):
        for i in range(2):
            part_copy(phase, i).wait_send()
            for off in range(1, n_frq):
                piece_copy(phase, i, off).wait_send()
    piece_copy(2, 1, 0).wait_send()

    @pl.when(core == 0)
    def _():
        piece_copy(1, 1, 0).wait_send()


def on_device(n_blk, n_frq, spectra, channel_valid):
    freq_total = spectra.shape[3] * n_frq
    halves = spectra.reshape(2, CB, W, 2, K).transpose(3, 2, 0, 1, 4).reshape(2, W, 2 * CB, K)
    rows = CB // n_frq
    scale = 1.0 / (M * math.sqrt(W * CB * freq_total))
    vmem = pl.BlockSpec(memory_space=pltpu.VMEM)
    hbm = pl.BlockSpec(memory_space=pl.ANY)
    dma = pltpu.SemaphoreType.DMA
    fine, coarse = lag_tables(freq_total)
    stacked = pl.pallas_call(
        functools.partial(kernel, n_blk, n_frq),
        out_shape=jax.ShapeDtypeStruct((ROUNDS, rows, LAGS), jnp.float32),
        in_specs=[hbm, vmem, hbm, hbm, hbm, hbm],
        out_specs=vmem,
        scratch_shapes=[
            pltpu.VMEM((2, W, 2 * CB, K), jnp.bfloat16),
            pltpu.VMEM((2 * M, 2 * CB), jnp.bfloat16),
            pltpu.VMEM((2 * CB, 2 * M), jnp.bfloat16),
            pltpu.VMEM((2, K, TAU), jnp.float32),
            pltpu.VMEM((2, TAU), jnp.float32),
            pltpu.VMEM((2 * K, TAU), jnp.bfloat16),
            pltpu.VMEM((CB, K), jnp.float32),
            pltpu.VMEM((2, W, 2 * CB, K), jnp.bfloat16),
            pltpu.VMEM((3, W, 2, 2 * CB, K), jnp.bfloat16),
            pltpu.VMEM((3, W, 2 * M, 2 * K), jnp.float32),
            pltpu.VMEM((2, ROUNDS, 2 * M, K), jnp.float32),
            pltpu.VMEM((2, 2, CB, TAU), jnp.bfloat16),
            pltpu.VMEM((2, 2, CB, TAU), jnp.bfloat16),
            pltpu.VMEM((2, 2, CB, TAU), jnp.bfloat16),
            pltpu.VMEM((ROUNDS, n_frq, rows, TAU), jnp.bfloat16),
            dma((5,)),
            dma((W,)),
            dma((3, W, 2)),
            dma((3, W, 2)),
            dma((2, 2)),
            dma((2, 2)),
            dma((2, 2, n_frq)),
            dma((ROUNDS, n_frq)),
        ],
        compiler_params=pltpu.CompilerParams(collective_id=0, has_side_effects=True),
    )(
        halves,
        channel_valid.reshape(2, K),
        jnp.asarray(forward_table()),
        jnp.asarray(inverse_table(scale)),
        jnp.asarray(fine),
        jnp.asarray(coarse),
    )
    return stacked.transpose(0, 2, 1)[None]


def solution(mesh):
    return jax.shard_map(
        functools.partial(on_device, mesh.shape["blk"], mesh.shape["frq"]),
        mesh=mesh,
        in_specs=(P(None, "blk", None, "frq"), P("blk")),
        out_specs=P("blk", None, None, "frq"),
        check_vma=False,
    )
```

```python
import functools
import math

import jax
import jax.numpy as jnp
import ml_dtypes
import numpy as np
from jax import lax
from jax.experimental import pallas as pl
from jax.experimental.pallas import tpu as pltpu
from jax.sharding import PartitionSpec as P

LAGS = 201
ROUNDS = 4
CB = 256
W = 4
M = 384
K = 128
TAU = 256
EARLY = 3
MESH = pl.DeviceIdType.MESH


def forward_table():
    angle = 2.0 * np.pi / M * (np.outer(np.arange(M), np.arange(CB)) % M)
    cos, sin = np.cos(angle), np.sin(angle)
    return np.block([[cos, sin], [-sin, cos]]).astype(ml_dtypes.bfloat16)


def inverse_table(scale):
    angle = 2.0 * np.pi / M * (np.outer(np.arange(CB) - CB // 2, np.arange(M)) % M)
    cos, sin = scale * np.cos(angle), scale * np.sin(angle)
    return np.block([[cos, -sin], [sin, cos]]).astype(ml_dtypes.bfloat16)


def lag_tables(freq_total):
    lag = np.arange(TAU) - (LAGS - 1) // 2
    keep = np.arange(TAU) < LAGS

    def waves(freq):
        angle = np.pi / freq_total * (np.outer(freq, lag) % (2 * freq_total))
        return np.stack([np.where(keep, np.cos(angle), 0.0), np.where(keep, np.sin(angle), 0.0)])

    fine = waves(np.arange(K)).astype(np.float32)
    coarse = waves(np.arange(0, freq_total, K)).transpose(1, 0, 2).astype(np.float32)
    return fine, coarse


C, D, B, E, A, F = (0, 0), (0, 1), (1, 0), (1, 1), (2, 0), (2, 1)
PHASE_PAIRS = (
    ((C, B), (E, B), (D, C), (D, B)),
    ((C, A), (E, A), (D, A), (F, B)),
)


def kernel(
    n_blk, n_frq, raw_hbm, valid_ref, fwd_hbm, inv_hbm, fine_hbm, coarse_hbm, out_ref,
    raw, fwd, inv, fine, coarse, lag, column, mine, near, hats, acc, part_out, part_in, piece_out, piece_in,
    load_sem, local_sem, send_sem, recv_sem, part_send, part_recv, piece_send, piece_recv, ready,
):
    blk = lax.axis_index("blk")
    frq = lax.axis_index("frq")
    chips = n_blk // 2
    rows = CB // n_frq
    chip, core = blk // 2, blk % 2
    right = (chip + 1) % chips
    left = (chip + chips - 1) % chips
    partner = (chip * 2 + 1 - core, frq)

    loads = [
        pltpu.make_async_copy(raw_hbm, raw, load_sem.at[0]),
        pltpu.make_async_copy(fwd_hbm, fwd, load_sem.at[1]),
        pltpu.make_async_copy(inv_hbm, inv, load_sem.at[2]),
        pltpu.make_async_copy(fine_hbm, fine, load_sem.at[3]),
        pltpu.make_async_copy(coarse_hbm.at[frq * 2 + core], coarse, load_sem.at[4]),
    ]
    for copy in loads:
        copy.start()

    barrier = pltpu.get_barrier_semaphore()
    side = n_frq // 2
    next_x, last_x = frq // side * side + (frq + 1) % side, frq // side * side + (frq + side - 1) % side
    across = (frq + side) % n_frq
    peers = [partner, (blk, next_x), (blk, last_x), (blk, across)]
    for c in range(2):
        peers += [(right * 2 + c, frq), (left * 2 + c, frq)]
    for peer in peers:
        pl.semaphore_signal(barrier, inc=1, device_id=peer, device_id_type=MESH)

    here = lax.broadcasted_iota(jnp.int32, (K, K), 0) == lax.broadcasted_iota(jnp.int32, (K, K), 1)
    for part in range(CB // K):
        row = valid_ref[part : part + 1, :].astype(jnp.float32)
        spread = jnp.where(here, jnp.broadcast_to(row, (K, K)), 0.0)
        total = jnp.sum(spread, axis=1, keepdims=True)
        column[part * K : (part + 1) * K] = jnp.broadcast_to(total, (K, K))

    loads[0].wait()

    def whiten(t, carry):
        real = pl.ds(pl.multiple_of(t * 16, 16), 16)
        imag = pl.ds(pl.multiple_of(CB + t * 16, 16), 16)
        keep = column[real]
        for half in range(2):
            lanes = slice(half * K, (half + 1) * K)
            both = [jnp.swapaxes(raw[r, real, :, lanes].astype(jnp.float32), 0, 1) for r in range(2)]
            values = [(both[0][w], both[1][w]) for w in range(W)]
            power = sum(re * re + im * im for re, im in values) * (1.0 / W)
            factor = keep / jnp.maximum(jnp.sqrt(power), 0.5)
            for w, (re, im) in enumerate(values):
                mine[half, w, real] = (re * factor).astype(jnp.bfloat16)
                mine[half, w, imag] = (im * factor).astype(jnp.bfloat16)
        return carry

    lax.fori_loop(0, CB // 16, whiten, 0, unroll=2)
    pl.semaphore_wait(barrier, len(peers))

    def local_copy(w):
        return pltpu.make_async_copy(mine.at[core, w], near.at[0, w, core], local_sem.at[w])

    def partner_copy(w):
        return pltpu.make_async_remote_copy(
            src_ref=mine.at[1 - core, w],
            dst_ref=near.at[0, w, core],
            send_sem=send_sem.at[0, w, 0],
            recv_sem=recv_sem.at[0, w, core],
            device_id=partner,
            device_id_type=MESH,
        )

    def chip_copy(phase, w, half):
        rightward = core == (1 if phase == 1 else 0)
        side = 1 - core if phase == 1 else core
        return pltpu.make_async_remote_copy(
            src_ref=mine.at[half, w],
            dst_ref=near.at[phase, w, side],
            send_sem=send_sem.at[phase, w, half],
            recv_sem=recv_sem.at[phase, w, side],
            device_id=(jnp.where(rightward, right, left) * 2 + half, frq),
            device_id_type=MESH,
        )

    for w in range(W):
        for half in range(2):
            chip_copy(1, w, half).start()
        partner_copy(w).start()
        local_copy(w).start()

    for step, target in enumerate([(blk, last_x), (blk, across), (left * 2 + core, frq)]):
        pl.semaphore_signal(ready.at[step], inc=1, device_id=target, device_id_type=MESH)
        pl.semaphore_wait(ready.at[step], 1)

    acc[...] = jnp.zeros_like(acc)
    for copy in loads[1:]:
        copy.wait()
    fine_cos, fine_sin = fine[0], fine[1]
    coarse_cos, coarse_sin = coarse[0:1], coarse[1:2]
    lag[:K] = (fine_cos * coarse_cos - fine_sin * coarse_sin).astype(jnp.bfloat16)
    lag[K:] = (-(fine_sin * coarse_cos + fine_cos * coarse_sin)).astype(jnp.bfloat16)

    def wait_landed(slot, w, c):
        pltpu.make_async_copy(near.at[slot, w, c], near.at[slot, w, c], recv_sem.at[slot, w, c]).wait()

    def hat(slot, w):
        data = jnp.concatenate([near[slot, w, 0], near[slot, w, 1]], axis=1)
        hats[slot, w] = jnp.dot(fwd[...], data, preferred_element_type=jnp.float32)

    def cross(phase, w):
        pairs = PHASE_PAIRS[phase - 1]
        used = sorted({block for pair in pairs for block in pair})

        def tile(t, carry):
            re = pl.ds(pl.multiple_of(t * 8, 8), 8)
            im = pl.ds(pl.multiple_of(M + t * 8, 8), 8)
            value = {}
            for slot, c in used:
                lanes = slice(c * K, (c + 1) * K)
                value[slot, c] = (hats[slot, w, re, lanes], hats[slot, w, im, lanes])
            for index, (one, two) in enumerate(pairs):
                (ar, ai), (br, bi) = value[one], value[two]
                acc[phase - 1, index, re] += ar * br + ai * bi
                acc[phase - 1, index, im] += ai * br - ar * bi
            return carry

        lax.fori_loop(0, M // 8, tile, 0, unroll=2)

    def correlations(phase, index):
        both = jnp.concatenate([acc[phase - 1, index], acc[phase - 1, index + 1]], axis=1)
        stack = jnp.dot(inv[...], both.astype(jnp.bfloat16), preferred_element_type=jnp.float32)
        stack = stack.astype(jnp.bfloat16)
        for c in range(2):
            lanes = slice(c * K, (c + 1) * K)
            pair = jnp.concatenate([stack[:CB, lanes], stack[CB:, lanes]], axis=1)
            yield jnp.dot(pair, lag[...], preferred_element_type=jnp.float32)

    def part_copy(phase, i):
        return pltpu.make_async_remote_copy(
            src_ref=part_out.at[phase - 1, i],
            dst_ref=part_in.at[phase - 1, i],
            send_sem=part_send.at[phase - 1, i],
            recv_sem=part_recv.at[phase - 1, i],
            device_id=partner,
            device_id_type=MESH,
        )

    def place(phase, i):
        if phase == 1:
            return (0, 0) if i == 0 else (2 - core, 1 - core)
        return (1 + core, 0) if i == 0 else (3, 1)

    def piece_rows(other):
        return pl.ds(pl.multiple_of(other * rows, rows), rows)

    def piece_copy(phase, i, off):
        j, shift = place(phase, i)
        other = (frq + off) % n_frq
        return pltpu.make_async_remote_copy(
            src_ref=piece_out.at[phase - 1, i, piece_rows(other)],
            dst_ref=piece_in.at[j, frq],
            send_sem=piece_send.at[phase - 1, i, off],
            recv_sem=piece_recv.at[j, frq],
            device_id=((chip + shift) % chips * 2 + core, other),
            device_id_type=MESH,
        )

    def own_copy(phase, i):
        j, _ = place(phase, i)
        return pltpu.make_async_copy(
            piece_out.at[phase - 1, i, piece_rows(frq)], piece_in.at[j, frq], piece_recv.at[j, frq]
        )

    def scatter(phase):
        for i, value in enumerate(correlations(phase, (1 - core) * 2)):
            part_out[phase - 1, i] = value.astype(jnp.bfloat16)
            part_copy(phase, i).start()
        for i, value in enumerate(correlations(phase, core * 2)):
            part_copy(phase, i).wait_recv()
            both = value + part_in[phase - 1, i].astype(jnp.float32)
            piece_out[phase - 1, i] = both.astype(jnp.bfloat16)
            for off in range(1, n_frq):
                piece_copy(phase, i, off).start()
            if i == 0:
                own_copy(phase, i).start()
            elif phase == 2:
                piece_copy(phase, i, 0).start()
            else:
                @pl.when(core == 0)
                def _():
                    piece_copy(1, 1, 0).start()

                @pl.when(core == 1)
                def _():
                    own_copy(1, 1).start()

    def first(w, carry):
        local_copy(w).wait()
        wait_landed(0, w, 1 - core)
        hat(0, w)
        for c in range(2):
            wait_landed(1, w, c)
        hat(1, w)
        cross(1, w)
        return carry

    lax.fori_loop(0, EARLY, first, 0)
    for w in range(W):
        for half in range(2):
            chip_copy(2, w, half).start()
    lax.fori_loop(EARLY, W, first, 0)
    scatter(1)

    def second(w, carry):
        for c in range(2):
            wait_landed(2, w, c)
        hat(2, w)
        cross(2, w)
        return carry

    lax.fori_loop(0, W, second, 0)
    scatter(2)

    for j in range(ROUNDS):
        total = jnp.zeros((rows, TAU), jnp.float32)
        for f in range(n_frq):
            pltpu.make_async_copy(piece_in.at[j, f], piece_in.at[j, f], piece_recv.at[j, f]).wait()
            total += piece_in[j, f].astype(jnp.float32)
        total = jnp.where(blk > j, total, 0.0)
        out_ref[j] = total[:, :LAGS]

    for w in range(W):
        partner_copy(w).wait_send()
        for half in range(2):
            chip_copy(1, w, half).wait_send()
            chip_copy(2, w, half).wait_send()
    for phase in (1, 2):
        for i in range(2):
            part_copy(phase, i).wait_send()
            for off in range(1, n_frq):
                piece_copy(phase, i, off).wait_send()
    piece_copy(2, 1, 0).wait_send()

    @pl.when(core == 0)
    def _():
        piece_copy(1, 1, 0).wait_send()


def on_device(n_blk, n_frq, spectra, channel_valid):
    freq_total = spectra.shape[3] * n_frq
    rows = CB // n_frq
    scale = 1.0 / (M * math.sqrt(W * CB * freq_total))
    vmem = pl.BlockSpec(memory_space=pltpu.VMEM)
    hbm = pl.BlockSpec(memory_space=pl.ANY)
    dma = pltpu.SemaphoreType.DMA
    fine, coarse = lag_tables(freq_total)
    stacked = pl.pallas_call(
        functools.partial(kernel, n_blk, n_frq),
        out_shape=pltpu.VMEM((ROUNDS, rows, LAGS), jnp.float32),
        in_specs=[hbm, vmem, hbm, hbm, hbm, hbm],
        out_specs=vmem,
        scratch_shapes=[
            pltpu.VMEM((2, CB, W, 2 * K), jnp.bfloat16),
            pltpu.VMEM((2 * M, 2 * CB), jnp.bfloat16),
            pltpu.VMEM((2 * CB, 2 * M), jnp.bfloat16),
            pltpu.VMEM((2, K, TAU), jnp.float32),
            pltpu.VMEM((2, TAU), jnp.float32),
            pltpu.VMEM((2 * K, TAU), jnp.bfloat16),
            pltpu.VMEM((CB, K), jnp.float32),
            pltpu.VMEM((2, W, 2 * CB, K), jnp.bfloat16),
            pltpu.VMEM((3, W, 2, 2 * CB, K), jnp.bfloat16),
            pltpu.VMEM((3, W, 2 * M, 2 * K), jnp.float32),
            pltpu.VMEM((2, ROUNDS, 2 * M, K), jnp.float32),
            pltpu.VMEM((2, 2, CB, TAU), jnp.bfloat16),
            pltpu.VMEM((2, 2, CB, TAU), jnp.bfloat16),
            pltpu.VMEM((2, 2, CB, TAU), jnp.bfloat16),
            pltpu.VMEM((ROUNDS, n_frq, rows, TAU), jnp.bfloat16),
            dma((5,)),
            dma((W,)),
            dma((3, W, 2)),
            dma((3, W, 2)),
            dma((2, 2)),
            dma((2, 2)),
            dma((2, 2, n_frq)),
            dma((ROUNDS, n_frq)),
            pltpu.SemaphoreType.REGULAR((3,)),
        ],
        compiler_params=pltpu.CompilerParams(collective_id=0, has_side_effects=True),
    )(
        spectra,
        channel_valid.reshape(2, K),
        jnp.asarray(forward_table()),
        jnp.asarray(inverse_table(scale)),
        jnp.asarray(fine),
        jnp.asarray(coarse),
    )
    return stacked.transpose(0, 2, 1)[None]


def solution(mesh):
    return jax.shard_map(
        functools.partial(on_device, mesh.shape["blk"], mesh.shape["frq"]),
        mesh=mesh,
        in_specs=(P(None, "blk", None, "frq"), P("blk")),
        out_specs=P("blk", None, None, "frq"),
        check_vma=False,
    )
```

```python
import functools
import math

import jax
import jax.numpy as jnp
import ml_dtypes
import numpy as np
from jax import lax
from jax.experimental import pallas as pl
from jax.experimental.pallas import tpu as pltpu
from jax.sharding import PartitionSpec as P

LAGS = 201
ROUNDS = 4
CB = 256
W = 4
M = 384
K = 128
TAU = 256
PARTS = 4
PART = CB // PARTS
EARLY = 1
MESH = pl.DeviceIdType.MESH


def forward_table():
    angle = 2.0 * np.pi / M * (np.outer(np.arange(M), np.arange(CB)) % M)
    cos, sin = np.cos(angle), np.sin(angle)
    table = np.block([[cos, sin], [-sin, cos]])
    table = table.reshape(2 * M, 2, PARTS, PART).transpose(0, 2, 1, 3).reshape(2 * M, 2 * CB)
    return table.astype(ml_dtypes.bfloat16)


def inverse_table(scale):
    angle = 2.0 * np.pi / M * (np.outer(np.arange(CB) - CB // 2, np.arange(M)) % M)
    cos, sin = scale * np.cos(angle), scale * np.sin(angle)
    return np.block([[cos, -sin], [sin, cos]]).astype(ml_dtypes.bfloat16)


def lag_tables(freq_total):
    lag = np.arange(TAU) - (LAGS - 1) // 2
    keep = np.arange(TAU) < LAGS

    def waves(freq):
        angle = np.pi / freq_total * (np.outer(freq, lag) % (2 * freq_total))
        return np.stack([np.where(keep, np.cos(angle), 0.0), np.where(keep, np.sin(angle), 0.0)])

    fine = waves(np.arange(K)).astype(np.float32)
    coarse = waves(np.arange(0, freq_total, K)).transpose(1, 0, 2).astype(np.float32)
    return fine, coarse


C, D, B, E, A, F = (0, 0), (0, 1), (1, 0), (1, 1), (2, 0), (2, 1)
PHASE_PAIRS = (
    ((C, B), (E, B), (D, C), (D, B)),
    ((C, A), (E, A), (D, A), (F, B)),
)


def kernel(
    n_blk, n_frq, raw_hbm, valid_hbm, fwd_hbm, inv_hbm, fine_hbm, coarse_hbm, out_ref,
    raw, valid, fwd, inv, fine, coarse, lag, column, mine, near, hats, acc, part_out, part_in, piece_out, piece_in,
    load_sem, raw_sem, local_sem, send_sem, recv_sem, part_send, part_recv, piece_send, piece_recv, ready,
):
    blk = lax.axis_index("blk")
    frq = lax.axis_index("frq")
    chips = n_blk // 2
    rows = CB // n_frq
    chip, core = blk // 2, blk % 2
    right = (chip + 1) % chips
    left = (chip + chips - 1) % chips
    partner = (chip * 2 + 1 - core, frq)

    def raw_load(part):
        channels = pl.ds(part * PART, PART)
        return pltpu.make_async_copy(raw_hbm.at[:, channels], raw.at[:, channels], raw_sem.at[part])

    loads = [
        pltpu.make_async_copy(fwd_hbm, fwd, load_sem.at[0]),
        pltpu.make_async_copy(inv_hbm, inv, load_sem.at[1]),
        pltpu.make_async_copy(fine_hbm, fine, load_sem.at[2]),
        pltpu.make_async_copy(coarse_hbm.at[frq * 2 + core], coarse, load_sem.at[3]),
    ]
    valid_load = pltpu.make_async_copy(valid_hbm, valid, load_sem.at[4])
    valid_load.start()
    for part in range(PARTS):
        raw_load(part).start()

    barrier = pltpu.get_barrier_semaphore()
    side = n_frq // 2
    next_x, last_x = frq // side * side + (frq + 1) % side, frq // side * side + (frq + side - 1) % side
    across = (frq + side) % n_frq
    peers = [partner, (blk, next_x), (blk, last_x), (blk, across)]
    for c in range(2):
        peers += [(right * 2 + c, frq), (left * 2 + c, frq)]
    for peer in peers:
        pl.semaphore_signal(barrier, inc=1, device_id=peer, device_id_type=MESH)

    valid_load.wait()
    here = lax.broadcasted_iota(jnp.int32, (K, K), 0) == lax.broadcasted_iota(jnp.int32, (K, K), 1)
    for part in range(CB // K):
        row = valid[part : part + 1, :].astype(jnp.float32)
        spread = jnp.where(here, jnp.broadcast_to(row, (K, K)), 0.0)
        total = jnp.sum(spread, axis=1, keepdims=True)
        column[part * K : (part + 1) * K] = jnp.broadcast_to(total, (K, K))

    def whiten(part, t, carry):
        channels = pl.ds(pl.multiple_of(part * PART + t * 16, 16), 16)
        real = pl.ds(pl.multiple_of(2 * part * PART + t * 16, 16), 16)
        imag = pl.ds(pl.multiple_of((2 * part + 1) * PART + t * 16, 16), 16)
        keep = column[channels]
        for half in range(2):
            lanes = slice(half * K, (half + 1) * K)
            both = [jnp.swapaxes(raw[r, channels, :, lanes].astype(jnp.float32), 0, 1) for r in range(2)]
            values = [(both[0][w], both[1][w]) for w in range(W)]
            power = sum(re * re + im * im for re, im in values) * (1.0 / W)
            factor = keep / jnp.maximum(jnp.sqrt(power), 0.5)
            for w, (re, im) in enumerate(values):
                mine[half, w, real] = (re * factor).astype(jnp.bfloat16)
                mine[half, w, imag] = (im * factor).astype(jnp.bfloat16)
        return carry

    def local_copy(w):
        return pltpu.make_async_copy(mine.at[core, w], near.at[0, w, core], local_sem.at[w])

    def partner_copy(w):
        return pltpu.make_async_remote_copy(
            src_ref=mine.at[1 - core, w],
            dst_ref=near.at[0, w, core],
            send_sem=send_sem.at[0, w, 0],
            recv_sem=recv_sem.at[0, w, core],
            device_id=partner,
            device_id_type=MESH,
        )

    def chip_copy(phase, w, half):
        rightward = core == (1 if phase == 1 else 0)
        side = 1 - core if phase == 1 else core
        return pltpu.make_async_remote_copy(
            src_ref=mine.at[half, w],
            dst_ref=near.at[phase, w, side],
            send_sem=send_sem.at[phase, w, half],
            recv_sem=recv_sem.at[phase, w, side],
            device_id=(jnp.where(rightward, right, left) * 2 + half, frq),
            device_id_type=MESH,
        )

    def first_chunk(half, part):
        chunk = pl.ds(2 * part * PART, 2 * PART)
        return pltpu.make_async_remote_copy(
            src_ref=mine.at[half, 0, chunk],
            dst_ref=near.at[1, 0, 1 - core, chunk],
            send_sem=send_sem.at[1, 0, half],
            recv_sem=recv_sem.at[1, 0, 1 - core],
            device_id=(jnp.where(core == 1, right, left) * 2 + half, frq),
            device_id_type=MESH,
        )

    for part in range(PARTS):
        raw_load(part).wait()
        lax.fori_loop(0, PART // 16, functools.partial(whiten, part), 0, unroll=2)
        if part == 0:
            pl.semaphore_wait(barrier, len(peers))
        for half in range(2):
            first_chunk(half, part).start()
        if part == 0:
            for copy in loads:
                copy.start()
    for w in range(W):
        if w > 0:
            for half in range(2):
                chip_copy(1, w, half).start()
        partner_copy(w).start()
        local_copy(w).start()

    for step, target in enumerate([(blk, last_x), (blk, across), (left * 2 + core, frq)]):
        pl.semaphore_signal(ready.at[step], inc=1, device_id=target, device_id_type=MESH)
        pl.semaphore_wait(ready.at[step], 1)

    acc[...] = jnp.zeros_like(acc)
    for copy in loads:
        copy.wait()
    fine_cos, fine_sin = fine[0], fine[1]
    coarse_cos, coarse_sin = coarse[0:1], coarse[1:2]
    lag[:K] = (fine_cos * coarse_cos - fine_sin * coarse_sin).astype(jnp.bfloat16)
    lag[K:] = (-(fine_sin * coarse_cos + fine_cos * coarse_sin)).astype(jnp.bfloat16)

    def wait_landed(slot, w, c):
        pltpu.make_async_copy(near.at[slot, w, c], near.at[slot, w, c], recv_sem.at[slot, w, c]).wait()

    def hat(slot, w):
        data = jnp.concatenate([near[slot, w, 0], near[slot, w, 1]], axis=1)
        hats[slot, w] = jnp.dot(fwd[...], data, preferred_element_type=jnp.float32)

    def cross(phase, w):
        pairs = PHASE_PAIRS[phase - 1]
        used = sorted({block for pair in pairs for block in pair})

        def tile(t, carry):
            re = pl.ds(pl.multiple_of(t * 8, 8), 8)
            im = pl.ds(pl.multiple_of(M + t * 8, 8), 8)
            value = {}
            for slot, c in used:
                lanes = slice(c * K, (c + 1) * K)
                value[slot, c] = (hats[slot, w, re, lanes], hats[slot, w, im, lanes])
            for index, (one, two) in enumerate(pairs):
                (ar, ai), (br, bi) = value[one], value[two]
                acc[phase - 1, index, re] += ar * br + ai * bi
                acc[phase - 1, index, im] += ai * br - ar * bi
            return carry

        lax.fori_loop(0, M // 8, tile, 0, unroll=16)

    def correlations(phase, index):
        both = jnp.concatenate([acc[phase - 1, index], acc[phase - 1, index + 1]], axis=1)
        stack = jnp.dot(inv[...], both.astype(jnp.bfloat16), preferred_element_type=jnp.float32)
        stack = stack.astype(jnp.bfloat16)
        for c in range(2):
            lanes = slice(c * K, (c + 1) * K)
            pair = jnp.concatenate([stack[:CB, lanes], stack[CB:, lanes]], axis=1)
            yield jnp.dot(pair, lag[...], preferred_element_type=jnp.float32)

    def part_copy(phase, i):
        return pltpu.make_async_remote_copy(
            src_ref=part_out.at[phase - 1, i],
            dst_ref=part_in.at[phase - 1, i],
            send_sem=part_send.at[phase - 1, i],
            recv_sem=part_recv.at[phase - 1, i],
            device_id=partner,
            device_id_type=MESH,
        )

    def place(phase, i):
        if phase == 1:
            return (0, 0) if i == 0 else (2 - core, 1 - core)
        return (1 + core, 0) if i == 0 else (3, 1)

    def piece_rows(other):
        return pl.ds(pl.multiple_of(other * rows, rows), rows)

    def piece_copy(phase, i, off):
        j, shift = place(phase, i)
        other = (frq + off) % n_frq
        return pltpu.make_async_remote_copy(
            src_ref=piece_out.at[phase - 1, i, piece_rows(other)],
            dst_ref=piece_in.at[j, frq],
            send_sem=piece_send.at[phase - 1, i, off],
            recv_sem=piece_recv.at[j, frq],
            device_id=((chip + shift) % chips * 2 + core, other),
            device_id_type=MESH,
        )

    def own_copy(phase, i):
        j, _ = place(phase, i)
        return pltpu.make_async_copy(
            piece_out.at[phase - 1, i, piece_rows(frq)], piece_in.at[j, frq], piece_recv.at[j, frq]
        )

    def scatter(phase):
        for i, value in enumerate(correlations(phase, (1 - core) * 2)):
            part_out[phase - 1, i] = value.astype(jnp.bfloat16)
            part_copy(phase, i).start()
        for i, value in enumerate(correlations(phase, core * 2)):
            part_copy(phase, i).wait_recv()
            both = value + part_in[phase - 1, i].astype(jnp.float32)
            piece_out[phase - 1, i] = both.astype(jnp.bfloat16)
            for off in range(1, n_frq):
                piece_copy(phase, i, off).start()
            if i == 0:
                own_copy(phase, i).start()
            elif phase == 2:
                piece_copy(phase, i, 0).start()
            else:
                @pl.when(core == 0)
                def _():
                    piece_copy(1, 1, 0).start()

                @pl.when(core == 1)
                def _():
                    own_copy(1, 1).start()

    def first(w, carry):
        local_copy(w).wait()
        wait_landed(0, w, 1 - core)
        hat(0, w)
        for c in range(2):
            wait_landed(1, w, c)
        hat(1, w)
        cross(1, w)
        return carry

    lax.fori_loop(0, EARLY, first, 0)
    for w in range(W):
        for half in range(2):
            chip_copy(2, w, half).start()
    lax.fori_loop(EARLY, W, first, 0)
    scatter(1)

    def second(w, carry):
        for c in range(2):
            wait_landed(2, w, c)
        hat(2, w)
        cross(2, w)
        return carry

    lax.fori_loop(0, W, second, 0)
    scatter(2)

    for j in range(ROUNDS):
        total = jnp.zeros((rows, TAU), jnp.float32)
        for f in range(n_frq):
            pltpu.make_async_copy(piece_in.at[j, f], piece_in.at[j, f], piece_recv.at[j, f]).wait()
            total += piece_in[j, f].astype(jnp.float32)
        total = jnp.where(blk > j, total, 0.0)
        out_ref[j] = total[:, :LAGS]

    for w in range(W):
        partner_copy(w).wait_send()
        for half in range(2):
            chip_copy(1, w, half).wait_send()
            chip_copy(2, w, half).wait_send()
    for phase in (1, 2):
        for i in range(2):
            part_copy(phase, i).wait_send()
            for off in range(1, n_frq):
                piece_copy(phase, i, off).wait_send()
    piece_copy(2, 1, 0).wait_send()

    @pl.when(core == 0)
    def _():
        piece_copy(1, 1, 0).wait_send()


def on_device(n_blk, n_frq, spectra, channel_valid):
    freq_total = spectra.shape[3] * n_frq
    rows = CB // n_frq
    scale = 1.0 / (M * math.sqrt(W * CB * freq_total))
    vmem = pl.BlockSpec(memory_space=pltpu.VMEM)
    hbm = pl.BlockSpec(memory_space=pl.ANY)
    dma = pltpu.SemaphoreType.DMA
    fine, coarse = lag_tables(freq_total)
    stacked = pl.pallas_call(
        functools.partial(kernel, n_blk, n_frq),
        out_shape=pltpu.VMEM((ROUNDS, rows, LAGS), jnp.float32),
        in_specs=[hbm, hbm, hbm, hbm, hbm, hbm],
        out_specs=vmem,
        scratch_shapes=[
            pltpu.VMEM((2, CB, W, 2 * K), jnp.bfloat16),
            pltpu.VMEM((2, K), jnp.int32),
            pltpu.VMEM((2 * M, 2 * CB), jnp.bfloat16),
            pltpu.VMEM((2 * CB, 2 * M), jnp.bfloat16),
            pltpu.VMEM((2, K, TAU), jnp.float32),
            pltpu.VMEM((2, TAU), jnp.float32),
            pltpu.VMEM((2 * K, TAU), jnp.bfloat16),
            pltpu.VMEM((CB, K), jnp.float32),
            pltpu.VMEM((2, W, 2 * CB, K), jnp.bfloat16),
            pltpu.VMEM((3, W, 2, 2 * CB, K), jnp.bfloat16),
            pltpu.VMEM((3, W, 2 * M, 2 * K), jnp.float32),
            pltpu.VMEM((2, ROUNDS, 2 * M, K), jnp.float32),
            pltpu.VMEM((2, 2, CB, TAU), jnp.bfloat16),
            pltpu.VMEM((2, 2, CB, TAU), jnp.bfloat16),
            pltpu.VMEM((2, 2, CB, TAU), jnp.bfloat16),
            pltpu.VMEM((ROUNDS, n_frq, rows, TAU), jnp.bfloat16),
            dma((5,)),
            dma((PARTS,)),
            dma((W,)),
            dma((3, W, 2)),
            dma((3, W, 2)),
            dma((2, 2)),
            dma((2, 2)),
            dma((2, 2, n_frq)),
            dma((ROUNDS, n_frq)),
            pltpu.SemaphoreType.REGULAR((3,)),
        ],
        compiler_params=pltpu.CompilerParams(collective_id=0, has_side_effects=True),
    )(
        spectra,
        channel_valid.reshape(2, K),
        jnp.asarray(forward_table()),
        jnp.asarray(inverse_table(scale)),
        jnp.asarray(fine),
        jnp.asarray(coarse),
    )
    return stacked.transpose(0, 2, 1)[None]


def solution(mesh):
    return jax.shard_map(
        functools.partial(on_device, mesh.shape["blk"], mesh.shape["frq"]),
        mesh=mesh,
        in_specs=(P(None, "blk", None, "frq"), P("blk")),
        out_specs=P("blk", None, None, "frq"),
        check_vma=False,
    )
```

```python
import functools
import math

import jax
import jax.numpy as jnp
import ml_dtypes
import numpy as np
from jax import lax
from jax.experimental import pallas as pl
from jax.experimental.pallas import tpu as pltpu
from jax.sharding import PartitionSpec as P

LAGS = 201
ROUNDS = 4
CB = 256
W = 4
M = 384
K = 128
TAU = 256
PARTS = 4
PART = CB // PARTS
EARLY = 1
MESH = pl.DeviceIdType.MESH


def forward_table():
    angle = 2.0 * np.pi / M * (np.outer(np.arange(M), np.arange(CB)) % M)
    cos, sin = np.cos(angle), np.sin(angle)
    table = np.block([[cos, sin], [-sin, cos]])
    table = table.reshape(2 * M, 2, PARTS, PART).transpose(0, 2, 1, 3).reshape(2 * M, 2 * CB)
    return table.astype(ml_dtypes.bfloat16)


def inverse_table(scale):
    angle = 2.0 * np.pi / M * (np.outer(np.arange(CB) - CB // 2, np.arange(M)) % M)
    cos, sin = scale * np.cos(angle), scale * np.sin(angle)
    return np.block([[cos, -sin], [sin, cos]]).astype(ml_dtypes.bfloat16)


def lag_tables(freq_total):
    lag = np.arange(TAU) - (LAGS - 1) // 2
    keep = np.arange(TAU) < LAGS

    def waves(freq):
        angle = np.pi / freq_total * (np.outer(freq, lag) % (2 * freq_total))
        return np.stack([np.where(keep, np.cos(angle), 0.0), np.where(keep, np.sin(angle), 0.0)])

    fine = waves(np.arange(K)).astype(np.float32)
    coarse = waves(np.arange(0, freq_total, K)).transpose(1, 0, 2).astype(np.float32)
    return fine, coarse


C, D, B, E, A, F = (0, 0), (0, 1), (1, 0), (1, 1), (2, 0), (2, 1)
PHASE_PAIRS = (
    ((C, B), (E, B), (D, C), (D, B)),
    ((C, A), (E, A), (D, A), (F, B)),
)


def kernel(
    n_blk, n_frq, raw_hbm, valid_hbm, fwd_hbm, inv_hbm, fine_hbm, coarse_hbm, out_ref,
    raw, valid, fwd, inv, fine, coarse, lag, column, mine, near, hats, acc, part_out, part_in, piece_out, piece_in,
    load_sem, raw_sem, local_sem, send_sem, recv_sem, part_send, part_recv, piece_send, piece_recv, ready,
):
    blk = lax.axis_index("blk")
    frq = lax.axis_index("frq")
    chips = n_blk // 2
    rows = CB // n_frq
    chip, core = blk // 2, blk % 2
    right = (chip + 1) % chips
    left = (chip + chips - 1) % chips
    partner = (chip * 2 + 1 - core, frq)

    def raw_load(part):
        channels = pl.ds(part * PART, PART)
        return pltpu.make_async_copy(raw_hbm.at[:, channels], raw.at[:, channels], raw_sem.at[part])

    loads = [
        pltpu.make_async_copy(fwd_hbm, fwd, load_sem.at[0]),
        pltpu.make_async_copy(inv_hbm, inv, load_sem.at[1]),
        pltpu.make_async_copy(fine_hbm, fine, load_sem.at[2]),
        pltpu.make_async_copy(coarse_hbm.at[frq * 2 + core], coarse, load_sem.at[3]),
    ]
    valid_load = pltpu.make_async_copy(valid_hbm, valid, load_sem.at[4])
    valid_load.start()
    for part in range(PARTS):
        raw_load(part).start()

    barrier = pltpu.get_barrier_semaphore()
    side = n_frq // 2
    next_x, last_x = frq // side * side + (frq + 1) % side, frq // side * side + (frq + side - 1) % side
    across = (frq + side) % n_frq
    peers = [partner, (blk, next_x), (blk, last_x), (blk, across)]
    for c in range(2):
        peers += [(right * 2 + c, frq), (left * 2 + c, frq)]
    for peer in peers:
        pl.semaphore_signal(barrier, inc=1, device_id=peer, device_id_type=MESH)

    valid_load.wait()
    here = lax.broadcasted_iota(jnp.int32, (K, K), 0) == lax.broadcasted_iota(jnp.int32, (K, K), 1)
    for part in range(CB // K):
        row = valid[part : part + 1, :].astype(jnp.float32)
        spread = jnp.where(here, jnp.broadcast_to(row, (K, K)), 0.0)
        total = jnp.sum(spread, axis=1, keepdims=True)
        column[part * K : (part + 1) * K] = jnp.broadcast_to(total, (K, K))

    def whiten(part, t, carry):
        channels = pl.ds(pl.multiple_of(part * PART + t * 16, 16), 16)
        real = pl.ds(pl.multiple_of(2 * part * PART + t * 16, 16), 16)
        imag = pl.ds(pl.multiple_of((2 * part + 1) * PART + t * 16, 16), 16)
        keep = column[channels]
        for half in range(2):
            lanes = slice(half * K, (half + 1) * K)
            both = [jnp.swapaxes(raw[r, channels, :, lanes].astype(jnp.float32), 0, 1) for r in range(2)]
            values = [(both[0][w], both[1][w]) for w in range(W)]
            power = sum(re * re + im * im for re, im in values) * (1.0 / W)
            factor = keep / jnp.maximum(jnp.sqrt(power), 0.5)
            for w, (re, im) in enumerate(values):
                mine[half, w, real] = (re * factor).astype(jnp.bfloat16)
                mine[half, w, imag] = (im * factor).astype(jnp.bfloat16)
        return carry

    def local_copy(w):
        return pltpu.make_async_copy(mine.at[core, w], near.at[0, w, core], local_sem.at[w])

    def partner_copy(w):
        return pltpu.make_async_remote_copy(
            src_ref=mine.at[1 - core, w],
            dst_ref=near.at[0, w, core],
            send_sem=send_sem.at[0, w, 0],
            recv_sem=recv_sem.at[0, w, core],
            device_id=partner,
            device_id_type=MESH,
        )

    def chip_copy(phase, w, half):
        rightward = core == (1 if phase == 1 else 0)
        side = 1 - core if phase == 1 else core
        return pltpu.make_async_remote_copy(
            src_ref=mine.at[half, w],
            dst_ref=near.at[phase, w, side],
            send_sem=send_sem.at[phase, w, half],
            recv_sem=recv_sem.at[phase, w, side],
            device_id=(jnp.where(rightward, right, left) * 2 + half, frq),
            device_id_type=MESH,
        )

    def first_chunk(half, part):
        chunk = pl.ds(2 * part * PART, 2 * PART)
        return pltpu.make_async_remote_copy(
            src_ref=mine.at[half, 0, chunk],
            dst_ref=near.at[1, 0, 1 - core, chunk],
            send_sem=send_sem.at[1, 0, half],
            recv_sem=recv_sem.at[1, 0, 1 - core],
            device_id=(jnp.where(core == 1, right, left) * 2 + half, frq),
            device_id_type=MESH,
        )

    for part in range(PARTS):
        raw_load(part).wait()
        lax.fori_loop(0, PART // 16, functools.partial(whiten, part), 0, unroll=2)
        if part == 0:
            pl.semaphore_wait(barrier, len(peers))
        for half in range(2):
            first_chunk(half, part).start()
        if part == 0:
            for copy in loads:
                copy.start()
    for w in range(W):
        if w > 0:
            for half in range(2):
                chip_copy(1, w, half).start()
        partner_copy(w).start()
        local_copy(w).start()

    for step, target in enumerate([(blk, last_x), (blk, across), (left * 2 + core, frq)]):
        pl.semaphore_signal(ready.at[step], inc=1, device_id=target, device_id_type=MESH)
        pl.semaphore_wait(ready.at[step], 1)

    acc[...] = jnp.zeros_like(acc)
    for copy in loads:
        copy.wait()
    fine_cos, fine_sin = fine[0], fine[1]
    coarse_cos, coarse_sin = coarse[0:1], coarse[1:2]
    lag[:K] = (fine_cos * coarse_cos - fine_sin * coarse_sin).astype(jnp.bfloat16)
    lag[K:] = (-(fine_sin * coarse_cos + fine_cos * coarse_sin)).astype(jnp.bfloat16)

    def wait_landed(slot, w, c):
        pltpu.make_async_copy(near.at[slot, w, c], near.at[slot, w, c], recv_sem.at[slot, w, c]).wait()

    def hat(slot, w):
        data = jnp.concatenate([near[slot, w, 0], near[slot, w, 1]], axis=1)
        hats[slot, w] = jnp.dot(fwd[...], data, preferred_element_type=jnp.float32)

    def cross(phase, w):
        pairs = PHASE_PAIRS[phase - 1]
        used = sorted({block for pair in pairs for block in pair})

        def tile(t, carry):
            re = pl.ds(pl.multiple_of(t * 8, 8), 8)
            im = pl.ds(pl.multiple_of(M + t * 8, 8), 8)
            value = {}
            for slot, c in used:
                lanes = slice(c * K, (c + 1) * K)
                value[slot, c] = (hats[slot, w, re, lanes], hats[slot, w, im, lanes])
            for index, (one, two) in enumerate(pairs):
                (ar, ai), (br, bi) = value[one], value[two]
                acc[phase - 1, index, re] += ar * br + ai * bi
                acc[phase - 1, index, im] += ai * br - ar * bi
            return carry

        lax.fori_loop(0, M // 8, tile, 0, unroll=16)

    def correlations(phase, index):
        both = jnp.concatenate([acc[phase - 1, index], acc[phase - 1, index + 1]], axis=1)
        stack = jnp.dot(inv[...], both.astype(jnp.bfloat16), preferred_element_type=jnp.float32)
        stack = stack.astype(jnp.bfloat16)
        for c in (1, 0):
            lanes = slice(c * K, (c + 1) * K)
            pair = jnp.concatenate([stack[:CB, lanes], stack[CB:, lanes]], axis=1)
            yield c, jnp.dot(pair, lag[...], preferred_element_type=jnp.float32)

    def part_copy(phase, i):
        return pltpu.make_async_remote_copy(
            src_ref=part_out.at[phase - 1, i],
            dst_ref=part_in.at[phase - 1, i],
            send_sem=part_send.at[phase - 1, i],
            recv_sem=part_recv.at[phase - 1, i],
            device_id=partner,
            device_id_type=MESH,
        )

    def place(phase, i):
        if phase == 1:
            return (0, 0) if i == 0 else (2 - core, 1 - core)
        return (1 + core, 0) if i == 0 else (3, 1)

    order = [half_off * side + off_x for half_off in (1, 0) for off_x in (2, 1, 3, 0)][:-1]

    def piece_rows(other):
        return pl.ds(pl.multiple_of(other * rows, rows), rows)

    def piece_copy(phase, i, off):
        j, shift = place(phase, i)
        half_off, off_x = divmod(off, side)
        other = ((frq // side + half_off) % 2) * side + (frq + off_x) % side
        return pltpu.make_async_remote_copy(
            src_ref=piece_out.at[phase - 1, i, piece_rows(other)],
            dst_ref=piece_in.at[j, frq],
            send_sem=piece_send.at[phase - 1, i, off],
            recv_sem=piece_recv.at[j, frq],
            device_id=((chip + shift) % chips * 2 + core, other),
            device_id_type=MESH,
        )

    def own_copy(phase, i):
        j, _ = place(phase, i)
        return pltpu.make_async_copy(
            piece_out.at[phase - 1, i, piece_rows(frq)], piece_in.at[j, frq], piece_recv.at[j, frq]
        )

    def scatter(phase):
        for i, value in correlations(phase, (1 - core) * 2):
            part_out[phase - 1, i] = value.astype(jnp.bfloat16)
            part_copy(phase, i).start()
        for i, value in correlations(phase, core * 2):
            part_copy(phase, i).wait_recv()
            both = value + part_in[phase - 1, i].astype(jnp.float32)
            piece_out[phase - 1, i] = both.astype(jnp.bfloat16)
            for off in order:
                piece_copy(phase, i, off).start()
            if i == 0:
                own_copy(phase, i).start()
            elif phase == 2:
                piece_copy(phase, i, 0).start()
            else:
                @pl.when(core == 0)
                def _():
                    piece_copy(1, 1, 0).start()

                @pl.when(core == 1)
                def _():
                    own_copy(1, 1).start()

    def first(w, carry):
        local_copy(w).wait()
        wait_landed(0, w, 1 - core)
        hat(0, w)
        for c in range(2):
            wait_landed(1, w, c)
        hat(1, w)
        cross(1, w)
        return carry

    lax.fori_loop(0, EARLY, first, 0)
    for w in range(W):
        for half in range(2):
            chip_copy(2, w, half).start()
    lax.fori_loop(EARLY, W, first, 0)
    scatter(1)

    def second(w, carry):
        for c in range(2):
            wait_landed(2, w, c)
        hat(2, w)
        cross(2, w)
        return carry

    lax.fori_loop(0, W, second, 0)
    scatter(2)

    for j in range(ROUNDS):
        total = jnp.zeros((rows, TAU), jnp.float32)
        for f in range(n_frq):
            pltpu.make_async_copy(piece_in.at[j, f], piece_in.at[j, f], piece_recv.at[j, f]).wait()
            total += piece_in[j, f].astype(jnp.float32)
        total = jnp.where(blk > j, total, 0.0)
        out_ref[j] = total[:, :LAGS]

    for w in range(W):
        partner_copy(w).wait_send()
        for half in range(2):
            chip_copy(1, w, half).wait_send()
            chip_copy(2, w, half).wait_send()
    for phase in (1, 2):
        for i in range(2):
            part_copy(phase, i).wait_send()
            for off in range(1, n_frq):
                piece_copy(phase, i, off).wait_send()
    piece_copy(2, 1, 0).wait_send()

    @pl.when(core == 0)
    def _():
        piece_copy(1, 1, 0).wait_send()


def on_device(n_blk, n_frq, spectra, channel_valid):
    freq_total = spectra.shape[3] * n_frq
    rows = CB // n_frq
    scale = 1.0 / (M * math.sqrt(W * CB * freq_total))
    vmem = pl.BlockSpec(memory_space=pltpu.VMEM)
    hbm = pl.BlockSpec(memory_space=pl.ANY)
    dma = pltpu.SemaphoreType.DMA
    fine, coarse = lag_tables(freq_total)
    stacked = pl.pallas_call(
        functools.partial(kernel, n_blk, n_frq),
        out_shape=pltpu.VMEM((ROUNDS, rows, LAGS), jnp.float32),
        in_specs=[hbm, hbm, hbm, hbm, hbm, hbm],
        out_specs=vmem,
        scratch_shapes=[
            pltpu.VMEM((2, CB, W, 2 * K), jnp.bfloat16),
            pltpu.VMEM((2, K), jnp.int32),
            pltpu.VMEM((2 * M, 2 * CB), jnp.bfloat16),
            pltpu.VMEM((2 * CB, 2 * M), jnp.bfloat16),
            pltpu.VMEM((2, K, TAU), jnp.float32),
            pltpu.VMEM((2, TAU), jnp.float32),
            pltpu.VMEM((2 * K, TAU), jnp.bfloat16),
            pltpu.VMEM((CB, K), jnp.float32),
            pltpu.VMEM((2, W, 2 * CB, K), jnp.bfloat16),
            pltpu.VMEM((3, W, 2, 2 * CB, K), jnp.bfloat16),
            pltpu.VMEM((3, W, 2 * M, 2 * K), jnp.float32),
            pltpu.VMEM((2, ROUNDS, 2 * M, K), jnp.float32),
            pltpu.VMEM((2, 2, CB, TAU), jnp.bfloat16),
            pltpu.VMEM((2, 2, CB, TAU), jnp.bfloat16),
            pltpu.VMEM((2, 2, CB, TAU), jnp.bfloat16),
            pltpu.VMEM((ROUNDS, n_frq, rows, TAU), jnp.bfloat16),
            dma((5,)),
            dma((PARTS,)),
            dma((W,)),
            dma((3, W, 2)),
            dma((3, W, 2)),
            dma((2, 2)),
            dma((2, 2)),
            dma((2, 2, n_frq)),
            dma((ROUNDS, n_frq)),
            pltpu.SemaphoreType.REGULAR((3,)),
        ],
        compiler_params=pltpu.CompilerParams(collective_id=0, has_side_effects=True),
    )(
        spectra,
        channel_valid.reshape(2, K),
        jnp.asarray(forward_table()),
        jnp.asarray(inverse_table(scale)),
        jnp.asarray(fine),
        jnp.asarray(coarse),
    )
    return stacked.transpose(0, 2, 1)[None]


def solution(mesh):
    return jax.shard_map(
        functools.partial(on_device, mesh.shape["blk"], mesh.shape["frq"]),
        mesh=mesh,
        in_specs=(P(None, "blk", None, "frq"), P("blk")),
        out_specs=P("blk", None, None, "frq"),
        check_vma=False,
    )
```

```python
import functools
import math

import jax
import jax.numpy as jnp
import ml_dtypes
import numpy as np
from jax import lax
from jax.experimental import pallas as pl
from jax.experimental.pallas import tpu as pltpu
from jax.sharding import PartitionSpec as P

LAGS = 201
ROUNDS = 4
CB = 256
W = 4
M = 384
K = 128
TAU = 256
PARTS = 4
PART = CB // PARTS
EARLY = 1
MESH = pl.DeviceIdType.MESH


def forward_table():
    angle = 2.0 * np.pi / M * (np.outer(np.arange(M), np.arange(CB)) % M)
    cos, sin = np.cos(angle), np.sin(angle)
    table = np.block([[cos, sin], [-sin, cos]])
    table = table.reshape(2 * M, 2, PARTS, PART).transpose(0, 2, 1, 3).reshape(2 * M, 2 * CB)
    return table.astype(ml_dtypes.bfloat16)


def inverse_table(scale):
    angle = 2.0 * np.pi / M * (np.outer(np.arange(CB) - CB // 2, np.arange(M)) % M)
    cos, sin = scale * np.cos(angle), scale * np.sin(angle)
    return np.block([[cos, -sin], [sin, cos]]).astype(ml_dtypes.bfloat16)


def lag_tables(freq_total):
    lag = np.arange(TAU) - (LAGS - 1) // 2
    keep = np.arange(TAU) < LAGS

    def waves(freq):
        angle = np.pi / freq_total * (np.outer(freq, lag) % (2 * freq_total))
        return np.stack([np.where(keep, np.cos(angle), 0.0), np.where(keep, np.sin(angle), 0.0)])

    fine = waves(np.arange(K)).astype(np.float32)
    coarse = waves(np.arange(0, freq_total, K)).transpose(1, 0, 2).astype(np.float32)
    return fine, coarse


C, D, B, E, A, F = (0, 0), (0, 1), (1, 0), (1, 1), (2, 0), (2, 1)
PHASE_PAIRS = (
    ((C, B), (E, B), (D, C), (D, B), (E, C)),
    (None, (E, A), (D, A), (F, B)),
)


def kernel(
    n_blk, n_frq, raw_hbm, valid_hbm, fwd_hbm, inv_hbm, fine_hbm, coarse_hbm, out_ref,
    raw, valid, fwd, inv, fine, coarse, lag, column, mine, near, hats, acc, part_out, part_in, piece_out, piece_in,
    load_sem, raw_sem, local_sem, send_sem, recv_sem, part_send, part_recv, piece_send, piece_recv, ready,
):
    blk = lax.axis_index("blk")
    frq = lax.axis_index("frq")
    chips = n_blk // 2
    rows = CB // n_frq
    chip, core = blk // 2, blk % 2
    right = (chip + 1) % chips
    left = (chip + chips - 1) % chips
    partner = (chip * 2 + 1 - core, frq)

    def raw_load(part):
        channels = pl.ds(part * PART, PART)
        return pltpu.make_async_copy(raw_hbm.at[:, channels], raw.at[:, channels], raw_sem.at[part])

    loads = [
        pltpu.make_async_copy(fwd_hbm, fwd, load_sem.at[0]),
        pltpu.make_async_copy(inv_hbm, inv, load_sem.at[1]),
        pltpu.make_async_copy(fine_hbm, fine, load_sem.at[2]),
        pltpu.make_async_copy(coarse_hbm.at[frq * 2 + core], coarse, load_sem.at[3]),
    ]
    valid_load = pltpu.make_async_copy(valid_hbm, valid, load_sem.at[4])
    valid_load.start()
    for part in range(PARTS):
        raw_load(part).start()

    barrier = pltpu.get_barrier_semaphore()
    side = n_frq // 2
    next_x, last_x = frq // side * side + (frq + 1) % side, frq // side * side + (frq + side - 1) % side
    across = (frq + side) % n_frq
    peers = [partner, (blk, next_x), (blk, last_x), (blk, across)]
    for c in range(2):
        peers += [(right * 2 + c, frq), (left * 2 + c, frq)]
    for peer in peers:
        pl.semaphore_signal(barrier, inc=1, device_id=peer, device_id_type=MESH)

    valid_load.wait()
    here = lax.broadcasted_iota(jnp.int32, (K, K), 0) == lax.broadcasted_iota(jnp.int32, (K, K), 1)
    for part in range(CB // K):
        row = valid[part : part + 1, :].astype(jnp.float32)
        spread = jnp.where(here, jnp.broadcast_to(row, (K, K)), 0.0)
        total = jnp.sum(spread, axis=1, keepdims=True)
        column[part * K : (part + 1) * K] = jnp.broadcast_to(total, (K, K))

    def whiten(part, t, carry):
        channels = pl.ds(pl.multiple_of(part * PART + t * 16, 16), 16)
        real = pl.ds(pl.multiple_of(2 * part * PART + t * 16, 16), 16)
        imag = pl.ds(pl.multiple_of((2 * part + 1) * PART + t * 16, 16), 16)
        keep = column[channels]
        for half in range(2):
            lanes = slice(half * K, (half + 1) * K)
            both = [jnp.swapaxes(raw[r, channels, :, lanes].astype(jnp.float32), 0, 1) for r in range(2)]
            values = [(both[0][w], both[1][w]) for w in range(W)]
            power = sum(re * re + im * im for re, im in values) * (1.0 / W)
            factor = keep / jnp.maximum(jnp.sqrt(power), 0.5)
            for w, (re, im) in enumerate(values):
                mine[half, w, real] = (re * factor).astype(jnp.bfloat16)
                mine[half, w, imag] = (im * factor).astype(jnp.bfloat16)
        return carry

    def local_copy(w):
        return pltpu.make_async_copy(mine.at[core, w], near.at[0, w, core], local_sem.at[w])

    def partner_copy(w):
        return pltpu.make_async_remote_copy(
            src_ref=mine.at[1 - core, w],
            dst_ref=near.at[0, w, core],
            send_sem=send_sem.at[0, w, 0],
            recv_sem=recv_sem.at[0, w, core],
            device_id=partner,
            device_id_type=MESH,
        )

    def chip_copy(phase, w, half):
        rightward = core == (1 if phase == 1 else 0)
        side = 1 - core if phase == 1 else core
        return pltpu.make_async_remote_copy(
            src_ref=mine.at[half, w],
            dst_ref=near.at[phase, w, side],
            send_sem=send_sem.at[phase, w, half],
            recv_sem=recv_sem.at[phase, w, side],
            device_id=(jnp.where(rightward, right, left) * 2 + half, frq),
            device_id_type=MESH,
        )

    def first_chunk(half, part):
        chunk = pl.ds(2 * part * PART, 2 * PART)
        return pltpu.make_async_remote_copy(
            src_ref=mine.at[half, 0, chunk],
            dst_ref=near.at[1, 0, 1 - core, chunk],
            send_sem=send_sem.at[1, 0, half],
            recv_sem=recv_sem.at[1, 0, 1 - core],
            device_id=(jnp.where(core == 1, right, left) * 2 + half, frq),
            device_id_type=MESH,
        )

    for part in range(PARTS):
        raw_load(part).wait()
        lax.fori_loop(0, PART // 16, functools.partial(whiten, part), 0, unroll=2)
        if part == 0:
            pl.semaphore_wait(barrier, len(peers))
        for half in range(2):
            first_chunk(half, part).start()
        if part == 0:
            for copy in loads:
                copy.start()
    for w in range(W):
        if w > 0:
            for half in range(2):
                chip_copy(1, w, half).start()
        partner_copy(w).start()
        local_copy(w).start()

    for step, target in enumerate([(blk, last_x), (blk, across), (left * 2 + core, frq)]):
        pl.semaphore_signal(ready.at[step], inc=1, device_id=target, device_id_type=MESH)
        pl.semaphore_wait(ready.at[step], 1)

    acc[...] = jnp.zeros_like(acc)
    for copy in loads:
        copy.wait()
    fine_cos, fine_sin = fine[0], fine[1]
    coarse_cos, coarse_sin = coarse[0:1], coarse[1:2]
    lag[:K] = (fine_cos * coarse_cos - fine_sin * coarse_sin).astype(jnp.bfloat16)
    lag[K:] = (-(fine_sin * coarse_cos + fine_cos * coarse_sin)).astype(jnp.bfloat16)

    def wait_landed(slot, w, c):
        pltpu.make_async_copy(near.at[slot, w, c], near.at[slot, w, c], recv_sem.at[slot, w, c]).wait()

    def hat(slot, w):
        data = jnp.concatenate([near[slot, w, 0], near[slot, w, 1]], axis=1)
        hats[slot, w] = jnp.dot(fwd[...], data, preferred_element_type=jnp.float32)

    def cross(phase, w):
        pairs = PHASE_PAIRS[phase - 1]
        used = sorted({block for pair in pairs if pair for block in pair})

        def tile(t, carry):
            re = pl.ds(pl.multiple_of(t * 8, 8), 8)
            im = pl.ds(pl.multiple_of(M + t * 8, 8), 8)
            value = {}
            for slot, c in used:
                lanes = slice(c * K, (c + 1) * K)
                value[slot, c] = (hats[slot, w, re, lanes], hats[slot, w, im, lanes])
            for index, pair in enumerate(pairs):
                if pair is None:
                    continue
                (ar, ai), (br, bi) = value[pair[0]], value[pair[1]]
                acc[phase - 1, index, re] += ar * br + ai * bi
                acc[phase - 1, index, im] += ai * br - ar * bi
            return carry

        lax.fori_loop(0, M // 8, tile, 0, unroll=16)

    def stacked_pairs(phase, index, count):
        both = jnp.concatenate([acc[phase - 1, index + c] for c in range(count)], axis=1)
        stack = jnp.dot(inv[...], both.astype(jnp.bfloat16), preferred_element_type=jnp.float32)
        stack = stack.astype(jnp.bfloat16)
        for c in reversed(range(count)):
            lanes = slice(c * K, (c + 1) * K)
            yield c, jnp.concatenate([stack[:CB, lanes], stack[CB:, lanes]], axis=1)

    def correlation(pair):
        return jnp.dot(pair, lag[...], preferred_element_type=jnp.float32)

    def part_copy(phase, i):
        return pltpu.make_async_remote_copy(
            src_ref=part_out.at[phase - 1, i],
            dst_ref=part_in.at[phase - 1, i],
            send_sem=part_send.at[phase - 1, i],
            recv_sem=part_recv.at[phase - 1, i],
            device_id=partner,
            device_id_type=MESH,
        )

    def place(phase, i):
        if phase == 1:
            return ((0, 0), (2 - core, 1 - core), (1, 1))[i]
        return (1 + core, 0) if i == 0 else (3, 1)

    order = [half_off * side + off_x for half_off in (1, 0) for off_x in (2, 1, 3, 0)][:-1]

    def piece_rows(other):
        return pl.ds(pl.multiple_of(other * rows, rows), rows)

    def piece_copy(phase, i, off):
        j, shift = place(phase, i)
        half_off, off_x = divmod(off, side)
        other = ((frq // side + half_off) % 2) * side + (frq + off_x) % side
        return pltpu.make_async_remote_copy(
            src_ref=piece_out.at[phase - 1, i, piece_rows(other)],
            dst_ref=piece_in.at[j, frq],
            send_sem=piece_send.at[phase - 1, i, off],
            recv_sem=piece_recv.at[j, frq],
            device_id=((chip + shift) % chips * 2 + core, other),
            device_id_type=MESH,
        )

    def own_copy(phase, i):
        j, _ = place(phase, i)
        return pltpu.make_async_copy(
            piece_out.at[phase - 1, i, piece_rows(frq)], piece_in.at[j, frq], piece_recv.at[j, frq]
        )

    def only(which):
        def run(body):
            if which is None:
                body()
            else:
                pl.when(core == which)(body)

        return run

    def reducer(phase, i):
        return {(1, 2): 0, (2, 0): 1}.get((phase, i))

    def other_core(which):
        return None if which is None else 1 - which

    def give_part(phase, i, pair):
        @only(other_core(reducer(phase, i)))
        def _():
            part_out[phase - 1, i] = correlation(pair).astype(jnp.bfloat16)
            part_copy(phase, i).start()

    def give_pieces(phase, i, pair):
        @only(reducer(phase, i))
        def _():
            value = correlation(pair)
            part_copy(phase, i).wait_recv()
            both = value + part_in[phase - 1, i].astype(jnp.float32)
            piece_out[phase - 1, i] = both.astype(jnp.bfloat16)
            for off in order:
                piece_copy(phase, i, off).start()
            if i == 0:
                own_copy(phase, i).start()
            elif (phase, i) != (1, 1):
                piece_copy(phase, i, 0).start()
            else:
                @pl.when(core == 0)
                def _():
                    piece_copy(1, 1, 0).start()

                @pl.when(core == 1)
                def _():
                    own_copy(1, 1).start()

    def scatter(phase):
        if phase == 1:
            @only(1)
            def _():
                for _, pair in stacked_pairs(1, 4, 1):
                    part_out[0, 2] = correlation(pair).astype(jnp.bfloat16)
                part_copy(1, 2).start()

        for i, pair in stacked_pairs(phase, (1 - core) * 2, 2):
            give_part(phase, i, pair)
        for i, pair in stacked_pairs(phase, core * 2, 2):
            give_pieces(phase, i, pair)
        if phase == 1:
            @only(0)
            def _():
                for _, pair in stacked_pairs(1, 4, 1):
                    value = correlation(pair)
                part_copy(1, 2).wait_recv()
                both = value + part_in[0, 2].astype(jnp.float32)
                piece_out[0, 2] = both.astype(jnp.bfloat16)
                for off in order + [0]:
                    piece_copy(1, 2, off).start()

    def first(w, carry):
        local_copy(w).wait()
        wait_landed(0, w, 1 - core)
        hat(0, w)
        for c in range(2):
            wait_landed(1, w, c)
        hat(1, w)
        cross(1, w)
        return carry

    lax.fori_loop(0, EARLY, first, 0)
    for w in range(W):
        for half in range(2):
            chip_copy(2, w, half).start()
    lax.fori_loop(EARLY, W, first, 0)
    scatter(1)

    def second(w, carry):
        for c in range(2):
            wait_landed(2, w, c)
        hat(2, w)
        cross(2, w)
        return carry

    lax.fori_loop(0, W, second, 0)
    scatter(2)

    for j in range(ROUNDS):
        total = jnp.zeros((rows, TAU), jnp.float32)
        for f in range(n_frq):
            pltpu.make_async_copy(piece_in.at[j, f], piece_in.at[j, f], piece_recv.at[j, f]).wait()
            total += piece_in[j, f].astype(jnp.float32)
        total = jnp.where(blk > j, total, 0.0)
        out_ref[j] = total[:, :LAGS]

    for w in range(W):
        partner_copy(w).wait_send()
        for half in range(2):
            chip_copy(1, w, half).wait_send()
            chip_copy(2, w, half).wait_send()
    for phase, i in ((1, 0), (1, 1), (1, 2), (2, 0), (2, 1)):
        @only(other_core(reducer(phase, i)))
        def _():
            part_copy(phase, i).wait_send()

        @only(reducer(phase, i))
        def _():
            for off in order:
                piece_copy(phase, i, off).wait_send()
            if (phase, i) in ((1, 2), (2, 1)):
                piece_copy(phase, i, 0).wait_send()

    @pl.when(core == 0)
    def _():
        piece_copy(1, 1, 0).wait_send()


def on_device(n_blk, n_frq, spectra, channel_valid):
    freq_total = spectra.shape[3] * n_frq
    rows = CB // n_frq
    scale = 1.0 / (M * math.sqrt(W * CB * freq_total))
    vmem = pl.BlockSpec(memory_space=pltpu.VMEM)
    hbm = pl.BlockSpec(memory_space=pl.ANY)
    dma = pltpu.SemaphoreType.DMA
    fine, coarse = lag_tables(freq_total)
    stacked = pl.pallas_call(
        functools.partial(kernel, n_blk, n_frq),
        out_shape=pltpu.VMEM((ROUNDS, rows, LAGS), jnp.float32),
        in_specs=[hbm, hbm, hbm, hbm, hbm, hbm],
        out_specs=vmem,
        scratch_shapes=[
            pltpu.VMEM((2, CB, W, 2 * K), jnp.bfloat16),
            pltpu.VMEM((2, K), jnp.int32),
            pltpu.VMEM((2 * M, 2 * CB), jnp.bfloat16),
            pltpu.VMEM((2 * CB, 2 * M), jnp.bfloat16),
            pltpu.VMEM((2, K, TAU), jnp.float32),
            pltpu.VMEM((2, TAU), jnp.float32),
            pltpu.VMEM((2 * K, TAU), jnp.bfloat16),
            pltpu.VMEM((CB, K), jnp.float32),
            pltpu.VMEM((2, W, 2 * CB, K), jnp.bfloat16),
            pltpu.VMEM((3, W, 2, 2 * CB, K), jnp.bfloat16),
            pltpu.VMEM((3, W, 2 * M, 2 * K), jnp.float32),
            pltpu.VMEM((2, 5, 2 * M, K), jnp.float32),
            pltpu.VMEM((2, 3, CB, TAU), jnp.bfloat16),
            pltpu.VMEM((2, 3, CB, TAU), jnp.bfloat16),
            pltpu.VMEM((2, 3, CB, TAU), jnp.bfloat16),
            pltpu.VMEM((ROUNDS, n_frq, rows, TAU), jnp.bfloat16),
            dma((5,)),
            dma((PARTS,)),
            dma((W,)),
            dma((3, W, 2)),
            dma((3, W, 2)),
            dma((2, 3)),
            dma((2, 3)),
            dma((2, 3, n_frq)),
            dma((ROUNDS, n_frq)),
            pltpu.SemaphoreType.REGULAR((3,)),
        ],
        compiler_params=pltpu.CompilerParams(collective_id=0, has_side_effects=True),
    )(
        spectra,
        channel_valid.reshape(2, K),
        jnp.asarray(forward_table()),
        jnp.asarray(inverse_table(scale)),
        jnp.asarray(fine),
        jnp.asarray(coarse),
    )
    return stacked.transpose(0, 2, 1)[None]


def solution(mesh):
    return jax.shard_map(
        functools.partial(on_device, mesh.shape["blk"], mesh.shape["frq"]),
        mesh=mesh,
        in_specs=(P(None, "blk", None, "frq"), P("blk")),
        out_specs=P("blk", None, None, "frq"),
        check_vma=False,
    )
```

```python
import functools
import math

import jax
import jax.numpy as jnp
import ml_dtypes
import numpy as np
from jax import lax
from jax.experimental import pallas as pl
from jax.experimental.pallas import tpu as pltpu
from jax.sharding import PartitionSpec as P

LAGS = 201
ROUNDS = 4
CB = 256
W = 4
M = 384
K = 128
TAU = 256
PARTS = 4
PART = CB // PARTS
EARLY = 1
MESH = pl.DeviceIdType.MESH


def forward_table():
    angle = 2.0 * np.pi / M * (np.outer(np.arange(M), np.arange(CB)) % M)
    cos, sin = np.cos(angle), np.sin(angle)
    table = np.block([[cos, sin], [-sin, cos]])
    table = table.reshape(2 * M, 2, PARTS, PART).transpose(0, 2, 1, 3).reshape(2 * M, 2 * CB)
    return table.astype(ml_dtypes.bfloat16)


def inverse_table(scale):
    angle = 2.0 * np.pi / M * (np.outer(np.arange(CB) - CB // 2, np.arange(M)) % M)
    cos, sin = scale * np.cos(angle), scale * np.sin(angle)
    return np.block([[cos, -sin], [sin, cos]]).astype(ml_dtypes.bfloat16)


def lag_tables(freq_total):
    lag = np.arange(TAU) - (LAGS - 1) // 2
    keep = np.arange(TAU) < LAGS

    def waves(freq):
        angle = np.pi / freq_total * (np.outer(freq, lag) % (2 * freq_total))
        return np.stack([np.where(keep, np.cos(angle), 0.0), np.where(keep, np.sin(angle), 0.0)])

    fine = waves(np.arange(K)).astype(np.float32)
    coarse = waves(np.arange(0, freq_total, K)).transpose(1, 0, 2).astype(np.float32)
    return fine, coarse


C, D, B, E, A, F = (0, 0), (0, 1), (1, 0), (1, 1), (2, 0), (2, 1)
PHASE_PAIRS = (
    ((C, B), (E, B), (D, C), (D, B), (E, C)),
    (None, (E, A), (D, A), (F, B)),
)


def kernel(
    n_blk, n_frq, raw_hbm, valid_hbm, fwd_hbm, inv_hbm, fine_hbm, coarse_hbm, out_ref,
    raw, valid, fwd, inv, fine, coarse, lag, column, mine, near, hats, acc, part_out, part_in, piece_out, piece_in,
    load_sem, raw_sem, local_sem, send_sem, recv_sem, part_send, part_recv, piece_send, piece_recv, ready,
):
    blk = lax.axis_index("blk")
    frq = lax.axis_index("frq")
    chips = n_blk // 2
    rows = CB // n_frq
    chip, core = blk // 2, blk % 2
    right = (chip + 1) % chips
    left = (chip + chips - 1) % chips
    partner = (chip * 2 + 1 - core, frq)
    has_left, has_right = chip > 0, chip < chips - 1

    def raw_load(part):
        channels = pl.ds(part * PART, PART)
        return pltpu.make_async_copy(raw_hbm.at[:, channels], raw.at[:, channels], raw_sem.at[part])

    loads = [
        pltpu.make_async_copy(fwd_hbm, fwd, load_sem.at[0]),
        pltpu.make_async_copy(inv_hbm, inv, load_sem.at[1]),
        pltpu.make_async_copy(fine_hbm, fine, load_sem.at[2]),
        pltpu.make_async_copy(coarse_hbm.at[frq * 2 + core], coarse, load_sem.at[3]),
    ]
    valid_load = pltpu.make_async_copy(valid_hbm, valid, load_sem.at[4])
    valid_load.start()
    for part in range(PARTS):
        raw_load(part).start()

    barrier = pltpu.get_barrier_semaphore()
    side = n_frq // 2
    next_x, last_x = frq // side * side + (frq + 1) % side, frq // side * side + (frq + side - 1) % side
    across = (frq + side) % n_frq
    peers = [partner, (blk, next_x), (blk, last_x), (blk, across)]

    def greet(devices):
        for device in devices:
            pl.semaphore_signal(barrier, inc=1, device_id=device, device_id_type=MESH)

    greet(peers)
    pl.when(has_left)(lambda: greet([(left * 2 + c, frq) for c in range(2)]))
    pl.when(has_right)(lambda: greet([(right * 2 + c, frq) for c in range(2)]))

    valid_load.wait()
    here = lax.broadcasted_iota(jnp.int32, (K, K), 0) == lax.broadcasted_iota(jnp.int32, (K, K), 1)
    for part in range(CB // K):
        row = valid[part : part + 1, :].astype(jnp.float32)
        spread = jnp.where(here, jnp.broadcast_to(row, (K, K)), 0.0)
        total = jnp.sum(spread, axis=1, keepdims=True)
        column[part * K : (part + 1) * K] = jnp.broadcast_to(total, (K, K))

    def whiten(part, t, carry):
        channels = pl.ds(pl.multiple_of(part * PART + t * 16, 16), 16)
        real = pl.ds(pl.multiple_of(2 * part * PART + t * 16, 16), 16)
        imag = pl.ds(pl.multiple_of((2 * part + 1) * PART + t * 16, 16), 16)
        keep = column[channels]
        for half in range(2):
            lanes = slice(half * K, (half + 1) * K)
            both = [jnp.swapaxes(raw[r, channels, :, lanes].astype(jnp.float32), 0, 1) for r in range(2)]
            values = [(both[0][w], both[1][w]) for w in range(W)]
            power = sum(re * re + im * im for re, im in values) * (1.0 / W)
            factor = keep / jnp.maximum(jnp.sqrt(power), 0.5)
            for w, (re, im) in enumerate(values):
                mine[half, w, real] = (re * factor).astype(jnp.bfloat16)
                mine[half, w, imag] = (im * factor).astype(jnp.bfloat16)
        return carry

    def local_copy(w):
        return pltpu.make_async_copy(mine.at[core, w], near.at[0, w, core], local_sem.at[w])

    def partner_copy(w):
        return pltpu.make_async_remote_copy(
            src_ref=mine.at[1 - core, w],
            dst_ref=near.at[0, w, core],
            send_sem=send_sem.at[0, w, 0],
            recv_sem=recv_sem.at[0, w, core],
            device_id=partner,
            device_id_type=MESH,
        )

    def chip_copy(phase, w, half):
        rightward = core == (1 if phase == 1 else 0)
        side = 1 - core if phase == 1 else core
        return pltpu.make_async_remote_copy(
            src_ref=mine.at[half, w],
            dst_ref=near.at[phase, w, side],
            send_sem=send_sem.at[phase, w, half],
            recv_sem=recv_sem.at[phase, w, side],
            device_id=(jnp.where(rightward, right, left) * 2 + half, frq),
            device_id_type=MESH,
        )

    def sends(phase):
        rightward = core == (1 if phase == 1 else 0)
        return (rightward & has_right) | (~rightward & has_left)

    def first_chunk(half, part):
        chunk = pl.ds(2 * part * PART, 2 * PART)
        return pltpu.make_async_remote_copy(
            src_ref=mine.at[half, 0, chunk],
            dst_ref=near.at[1, 0, 1 - core, chunk],
            send_sem=send_sem.at[1, 0, half],
            recv_sem=recv_sem.at[1, 0, 1 - core],
            device_id=(jnp.where(core == 1, right, left) * 2 + half, frq),
            device_id_type=MESH,
        )

    for part in range(PARTS):
        raw_load(part).wait()
        lax.fori_loop(0, PART // 16, functools.partial(whiten, part), 0, unroll=2)
        if part == 0:
            pl.semaphore_wait(
                barrier, len(peers) + jnp.where(has_left, 2, 0) + jnp.where(has_right, 2, 0)
            )
        @pl.when(sends(1))
        def _():
            for half in range(2):
                first_chunk(half, part).start()

        if part == 0:
            for copy in loads:
                copy.start()
    @pl.when(sends(1))
    def _():
        for w in range(1, W):
            for half in range(2):
                chip_copy(1, w, half).start()

    for w in range(W):
        partner_copy(w).start()
        local_copy(w).start()

    for step, target in enumerate([(blk, last_x), (blk, across)]):
        pl.semaphore_signal(ready.at[step], inc=1, device_id=target, device_id_type=MESH)
        pl.semaphore_wait(ready.at[step], 1)

    @pl.when(has_left)
    def _():
        pl.semaphore_signal(ready.at[2], inc=1, device_id=(left * 2 + core, frq), device_id_type=MESH)

    @pl.when(has_right)
    def _():
        pl.semaphore_wait(ready.at[2], 1)

    acc[...] = jnp.zeros_like(acc)
    for copy in loads:
        copy.wait()
    fine_cos, fine_sin = fine[0], fine[1]
    coarse_cos, coarse_sin = coarse[0:1], coarse[1:2]
    lag[:K] = (fine_cos * coarse_cos - fine_sin * coarse_sin).astype(jnp.bfloat16)
    lag[K:] = (-(fine_sin * coarse_cos + fine_cos * coarse_sin)).astype(jnp.bfloat16)

    def wait_landed(slot, w, c):
        pltpu.make_async_copy(near.at[slot, w, c], near.at[slot, w, c], recv_sem.at[slot, w, c]).wait()

    def wait_sides(slot, w):
        pl.when(has_left)(lambda: wait_landed(slot, w, 0))
        pl.when(has_right)(lambda: wait_landed(slot, w, 1))

    def hat(slot, w):
        data = jnp.concatenate([near[slot, w, 0], near[slot, w, 1]], axis=1)
        hats[slot, w] = jnp.dot(fwd[...], data, preferred_element_type=jnp.float32)

    def cross(phase, w):
        pairs = PHASE_PAIRS[phase - 1]
        used = sorted({block for pair in pairs if pair for block in pair})

        def tile(t, carry):
            re = pl.ds(pl.multiple_of(t * 8, 8), 8)
            im = pl.ds(pl.multiple_of(M + t * 8, 8), 8)
            value = {}
            for slot, c in used:
                lanes = slice(c * K, (c + 1) * K)
                value[slot, c] = (hats[slot, w, re, lanes], hats[slot, w, im, lanes])
            for index, pair in enumerate(pairs):
                if pair is None:
                    continue
                (ar, ai), (br, bi) = value[pair[0]], value[pair[1]]
                acc[phase - 1, index, re] += ar * br + ai * bi
                acc[phase - 1, index, im] += ai * br - ar * bi
            return carry

        lax.fori_loop(0, M // 8, tile, 0, unroll=16)

    def stacked_pairs(phase, index, count):
        both = jnp.concatenate([acc[phase - 1, index + c] for c in range(count)], axis=1)
        stack = jnp.dot(inv[...], both.astype(jnp.bfloat16), preferred_element_type=jnp.float32)
        stack = stack.astype(jnp.bfloat16)
        for c in reversed(range(count)):
            lanes = slice(c * K, (c + 1) * K)
            yield c, jnp.concatenate([stack[:CB, lanes], stack[CB:, lanes]], axis=1)

    def correlation(pair):
        return jnp.dot(pair, lag[...], preferred_element_type=jnp.float32)

    def part_copy(phase, i):
        return pltpu.make_async_remote_copy(
            src_ref=part_out.at[phase - 1, i],
            dst_ref=part_in.at[phase - 1, i],
            send_sem=part_send.at[phase - 1, i],
            recv_sem=part_recv.at[phase - 1, i],
            device_id=partner,
            device_id_type=MESH,
        )

    def place(phase, i):
        if phase == 1:
            return ((0, 0), (2 - core, 1 - core), (1, 1))[i]
        return (1 + core, 0) if i == 0 else (3, 1)

    order = [half_off * side + off_x for half_off in (1, 0) for off_x in (2, 1, 3, 0)][:-1]

    def piece_rows(other):
        return pl.ds(pl.multiple_of(other * rows, rows), rows)

    def piece_copy(phase, i, off):
        j, shift = place(phase, i)
        half_off, off_x = divmod(off, side)
        other = ((frq // side + half_off) % 2) * side + (frq + off_x) % side
        return pltpu.make_async_remote_copy(
            src_ref=piece_out.at[phase - 1, i, piece_rows(other)],
            dst_ref=piece_in.at[j, frq],
            send_sem=piece_send.at[phase - 1, i, off],
            recv_sem=piece_recv.at[j, frq],
            device_id=((chip + shift) % chips * 2 + core, other),
            device_id_type=MESH,
        )

    def own_copy(phase, i):
        j, _ = place(phase, i)
        return pltpu.make_async_copy(
            piece_out.at[phase - 1, i, piece_rows(frq)], piece_in.at[j, frq], piece_recv.at[j, frq]
        )

    def only(which):
        def run(body):
            if which is None:
                body()
            else:
                pl.when(core == which)(body)

        return run

    def reducer(phase, i):
        return {(1, 2): 0, (2, 0): 1}.get((phase, i))

    def other_core(which):
        return None if which is None else 1 - which

    def pieces(phase, i, act):
        def away():
            for off in order + [0]:
                act(piece_copy(phase, i, off))

        def here():
            for off in order:
                act(piece_copy(phase, i, off))

        if i == 0:
            here()
        elif (phase, i) != (1, 1):
            pl.when(has_right)(away)
        else:
            pl.when((core == 0) & has_right)(away)
            pl.when(core == 1)(here)

    def start_pieces(phase, i):
        pieces(phase, i, lambda copy: copy.start())
        if i == 0:
            own_copy(phase, i).start()
        elif (phase, i) == (1, 1):
            pl.when(core == 1)(lambda: own_copy(1, 1).start())

    def give_part(phase, i, pair):
        @only(other_core(reducer(phase, i)))
        def _():
            part_out[phase - 1, i] = correlation(pair).astype(jnp.bfloat16)
            part_copy(phase, i).start()

    def give_pieces(phase, i, pair):
        @only(reducer(phase, i))
        def _():
            value = correlation(pair)
            part_copy(phase, i).wait_recv()
            both = value + part_in[phase - 1, i].astype(jnp.float32)
            piece_out[phase - 1, i] = both.astype(jnp.bfloat16)
            start_pieces(phase, i)

    def scatter(phase):
        if phase == 1:
            @only(1)
            def _():
                for _, pair in stacked_pairs(1, 4, 1):
                    part_out[0, 2] = correlation(pair).astype(jnp.bfloat16)
                part_copy(1, 2).start()

        for i, pair in stacked_pairs(phase, (1 - core) * 2, 2):
            give_part(phase, i, pair)
        for i, pair in stacked_pairs(phase, core * 2, 2):
            give_pieces(phase, i, pair)
        if phase == 1:
            @only(0)
            def _():
                for _, pair in stacked_pairs(1, 4, 1):
                    value = correlation(pair)
                part_copy(1, 2).wait_recv()
                both = value + part_in[0, 2].astype(jnp.float32)
                piece_out[0, 2] = both.astype(jnp.bfloat16)
                start_pieces(1, 2)

    def first(w, carry):
        local_copy(w).wait()
        wait_landed(0, w, 1 - core)
        hat(0, w)
        wait_sides(1, w)
        hat(1, w)
        cross(1, w)
        return carry

    lax.fori_loop(0, EARLY, first, 0)

    @pl.when(sends(2))
    def _():
        for w in range(W):
            for half in range(2):
                chip_copy(2, w, half).start()

    lax.fori_loop(EARLY, W, first, 0)
    scatter(1)

    def second(w, carry):
        wait_sides(2, w)
        hat(2, w)
        cross(2, w)
        return carry

    lax.fori_loop(0, W, second, 0)
    scatter(2)

    for j in range(ROUNDS):
        total = jnp.zeros((rows, TAU), jnp.float32)
        come = True if j == 0 else has_left if j == 3 else (core == 1) | has_left

        @pl.when(come)
        def _():
            for f in range(n_frq):
                pltpu.make_async_copy(piece_in.at[j, f], piece_in.at[j, f], piece_recv.at[j, f]).wait()

        for f in range(n_frq):
            total += piece_in[j, f].astype(jnp.float32)
        total = jnp.where(blk > j, total, 0.0)
        out_ref[j] = total[:, :LAGS]

    for w in range(W):
        partner_copy(w).wait_send()
    for phase in (1, 2):
        @pl.when(sends(phase))
        def _():
            for w in range(W):
                for half in range(2):
                    chip_copy(phase, w, half).wait_send()

    for phase, i in ((1, 0), (1, 1), (1, 2), (2, 0), (2, 1)):
        @only(other_core(reducer(phase, i)))
        def _():
            part_copy(phase, i).wait_send()

        only(reducer(phase, i))(lambda: pieces(phase, i, lambda copy: copy.wait_send()))


def on_device(n_blk, n_frq, spectra, channel_valid):
    freq_total = spectra.shape[3] * n_frq
    rows = CB // n_frq
    scale = 1.0 / (M * math.sqrt(W * CB * freq_total))
    vmem = pl.BlockSpec(memory_space=pltpu.VMEM)
    hbm = pl.BlockSpec(memory_space=pl.ANY)
    dma = pltpu.SemaphoreType.DMA
    fine, coarse = lag_tables(freq_total)
    stacked = pl.pallas_call(
        functools.partial(kernel, n_blk, n_frq),
        out_shape=pltpu.VMEM((ROUNDS, rows, LAGS), jnp.float32),
        in_specs=[hbm, hbm, hbm, hbm, hbm, hbm],
        out_specs=vmem,
        scratch_shapes=[
            pltpu.VMEM((2, CB, W, 2 * K), jnp.bfloat16),
            pltpu.VMEM((2, K), jnp.int32),
            pltpu.VMEM((2 * M, 2 * CB), jnp.bfloat16),
            pltpu.VMEM((2 * CB, 2 * M), jnp.bfloat16),
            pltpu.VMEM((2, K, TAU), jnp.float32),
            pltpu.VMEM((2, TAU), jnp.float32),
            pltpu.VMEM((2 * K, TAU), jnp.bfloat16),
            pltpu.VMEM((CB, K), jnp.float32),
            pltpu.VMEM((2, W, 2 * CB, K), jnp.bfloat16),
            pltpu.VMEM((3, W, 2, 2 * CB, K), jnp.bfloat16),
            pltpu.VMEM((3, W, 2 * M, 2 * K), jnp.float32),
            pltpu.VMEM((2, 5, 2 * M, K), jnp.float32),
            pltpu.VMEM((2, 3, CB, TAU), jnp.bfloat16),
            pltpu.VMEM((2, 3, CB, TAU), jnp.bfloat16),
            pltpu.VMEM((2, 3, CB, TAU), jnp.bfloat16),
            pltpu.VMEM((ROUNDS, n_frq, rows, TAU), jnp.bfloat16),
            dma((5,)),
            dma((PARTS,)),
            dma((W,)),
            dma((3, W, 2)),
            dma((3, W, 2)),
            dma((2, 3)),
            dma((2, 3)),
            dma((2, 3, n_frq)),
            dma((ROUNDS, n_frq)),
            pltpu.SemaphoreType.REGULAR((3,)),
        ],
        compiler_params=pltpu.CompilerParams(collective_id=0, has_side_effects=True),
    )(
        spectra,
        channel_valid.reshape(2, K),
        jnp.asarray(forward_table()),
        jnp.asarray(inverse_table(scale)),
        jnp.asarray(fine),
        jnp.asarray(coarse),
    )
    return stacked.transpose(0, 2, 1)[None]


def solution(mesh):
    return jax.shard_map(
        functools.partial(on_device, mesh.shape["blk"], mesh.shape["frq"]),
        mesh=mesh,
        in_specs=(P(None, "blk", None, "frq"), P("blk")),
        out_specs=P("blk", None, None, "frq"),
        check_vma=False,
    )
```

```python
import functools
import math

import jax
import jax.numpy as jnp
import ml_dtypes
import numpy as np
from jax import lax
from jax.experimental import pallas as pl
from jax.experimental.pallas import tpu as pltpu
from jax.sharding import PartitionSpec as P

LAGS = 201
ROUNDS = 4
CB = 256
W = 4
M = 384
K = 128
TAU = 256
PARTS = 2
PART = CB // PARTS
EARLY = 1
MESH = pl.DeviceIdType.MESH


def forward_table():
    angle = 2.0 * np.pi / M * (np.outer(np.arange(M), np.arange(CB)) % M)
    cos, sin = np.cos(angle), np.sin(angle)
    table = np.block([[cos, sin], [-sin, cos]])
    table = table.reshape(2 * M, 2, PARTS, PART).transpose(0, 2, 1, 3).reshape(2 * M, 2 * CB)
    return table.astype(ml_dtypes.bfloat16)


def inverse_table(scale):
    angle = 2.0 * np.pi / M * (np.outer(np.arange(CB) - CB // 2, np.arange(M)) % M)
    cos, sin = scale * np.cos(angle), scale * np.sin(angle)
    return np.block([[cos, -sin], [sin, cos]]).astype(ml_dtypes.bfloat16)


def lag_tables(freq_total):
    lag = np.arange(TAU) - (LAGS - 1) // 2
    keep = np.arange(TAU) < LAGS

    def waves(freq):
        angle = np.pi / freq_total * (np.outer(freq, lag) % (2 * freq_total))
        return np.stack([np.where(keep, np.cos(angle), 0.0), np.where(keep, np.sin(angle), 0.0)])

    fine = waves(np.arange(K)).astype(np.float32)
    coarse = waves(np.arange(0, freq_total, K)).transpose(1, 0, 2).astype(np.float32)
    return fine, coarse


C, D, B, E, A, F = (0, 0), (0, 1), (1, 0), (1, 1), (2, 0), (2, 1)
PHASE_PAIRS = (
    ((C, B), (E, B), (D, C), (D, B), (E, C)),
    (None, (E, A), (D, A), (F, B)),
)


def kernel(
    n_blk, n_frq, raw_hbm, valid_hbm, fwd_hbm, inv_hbm, fine_hbm, coarse_hbm, out_ref,
    raw, valid, fwd, inv, fine, coarse, lag, column, mine, near, hats, acc, part_out, part_in, piece_out, piece_in,
    load_sem, raw_sem, local_sem, send_sem, recv_sem, part_send, part_recv, piece_send, piece_recv, ready,
):
    blk = lax.axis_index("blk")
    frq = lax.axis_index("frq")
    chips = n_blk // 2
    rows = CB // n_frq
    chip, core = blk // 2, blk % 2
    right = (chip + 1) % chips
    left = (chip + chips - 1) % chips
    partner = (chip * 2 + 1 - core, frq)
    has_left, has_right = chip > 0, chip < chips - 1

    def raw_load(part):
        channels = pl.ds(part * PART, PART)
        return pltpu.make_async_copy(raw_hbm.at[:, channels], raw.at[:, channels], raw_sem.at[part])

    loads = [
        pltpu.make_async_copy(fwd_hbm, fwd, load_sem.at[0]),
        pltpu.make_async_copy(inv_hbm, inv, load_sem.at[1]),
        pltpu.make_async_copy(fine_hbm, fine, load_sem.at[2]),
        pltpu.make_async_copy(coarse_hbm.at[frq * 2 + core], coarse, load_sem.at[3]),
    ]
    valid_load = pltpu.make_async_copy(valid_hbm, valid, load_sem.at[4])
    valid_load.start()
    for part in range(PARTS):
        raw_load(part).start()

    barrier = pltpu.get_barrier_semaphore()
    side = n_frq // 2
    next_x, last_x = frq // side * side + (frq + 1) % side, frq // side * side + (frq + side - 1) % side
    across = (frq + side) % n_frq
    peers = [partner, (blk, next_x), (blk, last_x), (blk, across)]

    def greet(devices):
        for device in devices:
            pl.semaphore_signal(barrier, inc=1, device_id=device, device_id_type=MESH)

    greet(peers)
    pl.when(has_left)(lambda: greet([(left * 2 + c, frq) for c in range(2)]))
    pl.when(has_right)(lambda: greet([(right * 2 + c, frq) for c in range(2)]))

    valid_load.wait()
    here = lax.broadcasted_iota(jnp.int32, (K, K), 0) == lax.broadcasted_iota(jnp.int32, (K, K), 1)
    for part in range(CB // K):
        row = valid[part : part + 1, :].astype(jnp.float32)
        spread = jnp.where(here, jnp.broadcast_to(row, (K, K)), 0.0)
        total = jnp.sum(spread, axis=1, keepdims=True)
        column[part * K : (part + 1) * K] = jnp.broadcast_to(total, (K, K))

    def whiten(part, t, carry):
        channels = pl.ds(pl.multiple_of(part * PART + t * 16, 16), 16)
        real = pl.ds(pl.multiple_of(2 * part * PART + t * 16, 16), 16)
        imag = pl.ds(pl.multiple_of((2 * part + 1) * PART + t * 16, 16), 16)
        keep = column[channels]
        for half in range(2):
            lanes = slice(half * K, (half + 1) * K)
            both = [jnp.swapaxes(raw[r, channels, :, lanes].astype(jnp.float32), 0, 1) for r in range(2)]
            values = [(both[0][w], both[1][w]) for w in range(W)]
            power = sum(re * re + im * im for re, im in values) * (1.0 / W)
            factor = keep / jnp.maximum(jnp.sqrt(power), 0.5)
            for w, (re, im) in enumerate(values):
                mine[half, w, real] = (re * factor).astype(jnp.bfloat16)
                mine[half, w, imag] = (im * factor).astype(jnp.bfloat16)
        return carry

    def local_copy(w):
        return pltpu.make_async_copy(mine.at[core, w], near.at[0, w, core], local_sem.at[w])

    def partner_copy(w):
        return pltpu.make_async_remote_copy(
            src_ref=mine.at[1 - core, w],
            dst_ref=near.at[0, w, core],
            send_sem=send_sem.at[0, w, 0],
            recv_sem=recv_sem.at[0, w, core],
            device_id=partner,
            device_id_type=MESH,
        )

    def chip_copy(phase, w, half):
        rightward = core == (1 if phase == 1 else 0)
        side = 1 - core if phase == 1 else core
        return pltpu.make_async_remote_copy(
            src_ref=mine.at[half, w],
            dst_ref=near.at[phase, w, side],
            send_sem=send_sem.at[phase, w, half],
            recv_sem=recv_sem.at[phase, w, side],
            device_id=(jnp.where(rightward, right, left) * 2 + half, frq),
            device_id_type=MESH,
        )

    def sends(phase):
        rightward = core == (1 if phase == 1 else 0)
        return (rightward & has_right) | (~rightward & has_left)

    def first_chunk(half, part):
        chunk = pl.ds(2 * part * PART, 2 * PART)
        return pltpu.make_async_remote_copy(
            src_ref=mine.at[half, 0, chunk],
            dst_ref=near.at[1, 0, 1 - core, chunk],
            send_sem=send_sem.at[1, 0, half],
            recv_sem=recv_sem.at[1, 0, 1 - core],
            device_id=(jnp.where(core == 1, right, left) * 2 + half, frq),
            device_id_type=MESH,
        )

    for part in range(PARTS):
        raw_load(part).wait()
        lax.fori_loop(0, PART // 16, functools.partial(whiten, part), 0, unroll=2)
        if part == 0:
            pl.semaphore_wait(
                barrier, len(peers) + jnp.where(has_left, 2, 0) + jnp.where(has_right, 2, 0)
            )
        @pl.when(sends(1))
        def _():
            for half in range(2):
                first_chunk(half, part).start()

        if part == 0:
            for copy in loads:
                copy.start()
    @pl.when(sends(1))
    def _():
        for w in range(1, W):
            for half in range(2):
                chip_copy(1, w, half).start()

    for w in range(W):
        partner_copy(w).start()
        local_copy(w).start()

    for step, target in enumerate([(blk, last_x), (blk, across)]):
        pl.semaphore_signal(ready.at[step], inc=1, device_id=target, device_id_type=MESH)
        pl.semaphore_wait(ready.at[step], 1)

    @pl.when(has_left)
    def _():
        pl.semaphore_signal(ready.at[2], inc=1, device_id=(left * 2 + core, frq), device_id_type=MESH)

    @pl.when(has_right)
    def _():
        pl.semaphore_wait(ready.at[2], 1)

    acc[...] = jnp.zeros_like(acc)
    for copy in loads:
        copy.wait()
    fine_cos, fine_sin = fine[0], fine[1]
    coarse_cos, coarse_sin = coarse[0:1], coarse[1:2]
    lag[:K] = (fine_cos * coarse_cos - fine_sin * coarse_sin).astype(jnp.bfloat16)
    lag[K:] = (-(fine_sin * coarse_cos + fine_cos * coarse_sin)).astype(jnp.bfloat16)

    def wait_landed(slot, w, c):
        pltpu.make_async_copy(near.at[slot, w, c], near.at[slot, w, c], recv_sem.at[slot, w, c]).wait()

    def wait_sides(slot, w):
        pl.when(has_left)(lambda: wait_landed(slot, w, 0))
        pl.when(has_right)(lambda: wait_landed(slot, w, 1))

    def hat(slot, w):
        data = jnp.concatenate([near[slot, w, 0], near[slot, w, 1]], axis=1)
        hats[slot, w] = jnp.dot(fwd[...], data, preferred_element_type=jnp.float32)

    def cross(phase, w):
        pairs = PHASE_PAIRS[phase - 1]
        used = sorted({block for pair in pairs if pair for block in pair})

        def tile(t, carry):
            re = pl.ds(pl.multiple_of(t * 8, 8), 8)
            im = pl.ds(pl.multiple_of(M + t * 8, 8), 8)
            value = {}
            for slot, c in used:
                lanes = slice(c * K, (c + 1) * K)
                value[slot, c] = (hats[slot, w, re, lanes], hats[slot, w, im, lanes])
            for index, pair in enumerate(pairs):
                if pair is None:
                    continue
                (ar, ai), (br, bi) = value[pair[0]], value[pair[1]]
                acc[phase - 1, index, re] += ar * br + ai * bi
                acc[phase - 1, index, im] += ai * br - ar * bi
            return carry

        lax.fori_loop(0, M // 8, tile, 0, unroll=16)

    def stacked_pairs(phase, index, count):
        both = jnp.concatenate([acc[phase - 1, index + c] for c in range(count)], axis=1)
        stack = jnp.dot(inv[...], both.astype(jnp.bfloat16), preferred_element_type=jnp.float32)
        stack = stack.astype(jnp.bfloat16)
        for c in reversed(range(count)):
            lanes = slice(c * K, (c + 1) * K)
            yield c, jnp.concatenate([stack[:CB, lanes], stack[CB:, lanes]], axis=1)

    def correlation(pair):
        return jnp.dot(pair, lag[...], preferred_element_type=jnp.float32)

    def part_copy(phase, i):
        return pltpu.make_async_remote_copy(
            src_ref=part_out.at[phase - 1, i],
            dst_ref=part_in.at[phase - 1, i],
            send_sem=part_send.at[phase - 1, i],
            recv_sem=part_recv.at[phase - 1, i],
            device_id=partner,
            device_id_type=MESH,
        )

    def place(phase, i):
        if phase == 1:
            return ((0, 0), (2 - core, 1 - core), (1, 1))[i]
        return (1 + core, 0) if i == 0 else (3, 1)

    order = [half_off * side + off_x for half_off in (1, 0) for off_x in (2, 1, 3, 0)][:-1]

    def piece_rows(other):
        return pl.ds(pl.multiple_of(other * rows, rows), rows)

    def piece_copy(phase, i, off):
        j, shift = place(phase, i)
        half_off, off_x = divmod(off, side)
        other = ((frq // side + half_off) % 2) * side + (frq + off_x) % side
        return pltpu.make_async_remote_copy(
            src_ref=piece_out.at[phase - 1, i, piece_rows(other)],
            dst_ref=piece_in.at[j, frq],
            send_sem=piece_send.at[phase - 1, i, off],
            recv_sem=piece_recv.at[j, frq],
            device_id=((chip + shift) % chips * 2 + core, other),
            device_id_type=MESH,
        )

    def own_copy(phase, i):
        j, _ = place(phase, i)
        return pltpu.make_async_copy(
            piece_out.at[phase - 1, i, piece_rows(frq)], piece_in.at[j, frq], piece_recv.at[j, frq]
        )

    def only(which):
        def run(body):
            if which is None:
                body()
            else:
                pl.when(core == which)(body)

        return run

    def reducer(phase, i):
        return {(1, 2): 0, (2, 0): 1}.get((phase, i))

    def other_core(which):
        return None if which is None else 1 - which

    def pieces(phase, i, act):
        def away():
            for off in order + [0]:
                act(piece_copy(phase, i, off))

        def here():
            for off in order:
                act(piece_copy(phase, i, off))

        if i == 0:
            here()
        elif (phase, i) != (1, 1):
            pl.when(has_right)(away)
        else:
            pl.when((core == 0) & has_right)(away)
            pl.when(core == 1)(here)

    def start_pieces(phase, i):
        pieces(phase, i, lambda copy: copy.start())
        if i == 0:
            own_copy(phase, i).start()
        elif (phase, i) == (1, 1):
            pl.when(core == 1)(lambda: own_copy(1, 1).start())

    def give_part(phase, i, pair):
        @only(other_core(reducer(phase, i)))
        def _():
            part_out[phase - 1, i] = correlation(pair).astype(jnp.bfloat16)
            part_copy(phase, i).start()

    def give_pieces(phase, i, pair):
        @only(reducer(phase, i))
        def _():
            value = correlation(pair)
            part_copy(phase, i).wait_recv()
            both = value + part_in[phase - 1, i].astype(jnp.float32)
            piece_out[phase - 1, i] = both.astype(jnp.bfloat16)
            start_pieces(phase, i)

    def scatter(phase):
        if phase == 1:
            @only(1)
            def _():
                for _, pair in stacked_pairs(1, 4, 1):
                    part_out[0, 2] = correlation(pair).astype(jnp.bfloat16)
                part_copy(1, 2).start()

        for i, pair in stacked_pairs(phase, (1 - core) * 2, 2):
            give_part(phase, i, pair)
        for i, pair in stacked_pairs(phase, core * 2, 2):
            give_pieces(phase, i, pair)
        if phase == 1:
            @only(0)
            def _():
                for _, pair in stacked_pairs(1, 4, 1):
                    value = correlation(pair)
                part_copy(1, 2).wait_recv()
                both = value + part_in[0, 2].astype(jnp.float32)
                piece_out[0, 2] = both.astype(jnp.bfloat16)
                start_pieces(1, 2)

    def first(w, carry):
        local_copy(w).wait()
        wait_landed(0, w, 1 - core)
        hat(0, w)
        wait_sides(1, w)
        hat(1, w)
        cross(1, w)
        return carry

    lax.fori_loop(0, EARLY, first, 0)

    @pl.when(sends(2))
    def _():
        for w in range(W):
            for half in range(2):
                chip_copy(2, w, half).start()

    lax.fori_loop(EARLY, W, first, 0)
    scatter(1)

    def second(w, carry):
        wait_sides(2, w)
        hat(2, w)
        cross(2, w)
        return carry

    lax.fori_loop(0, W, second, 0)
    scatter(2)

    for j in range(ROUNDS):
        total = jnp.zeros((rows, TAU), jnp.float32)
        come = True if j == 0 else has_left if j == 3 else (core == 1) | has_left

        @pl.when(come)
        def _():
            for f in range(n_frq):
                pltpu.make_async_copy(piece_in.at[j, f], piece_in.at[j, f], piece_recv.at[j, f]).wait()

        for f in range(n_frq):
            total += piece_in[j, f].astype(jnp.float32)
        total = jnp.where(blk > j, total, 0.0)
        out_ref[j] = total[:, :LAGS]

    for w in range(W):
        partner_copy(w).wait_send()
    for phase in (1, 2):
        @pl.when(sends(phase))
        def _():
            for w in range(W):
                for half in range(2):
                    chip_copy(phase, w, half).wait_send()

    for phase, i in ((1, 0), (1, 1), (1, 2), (2, 0), (2, 1)):
        @only(other_core(reducer(phase, i)))
        def _():
            part_copy(phase, i).wait_send()

        only(reducer(phase, i))(lambda: pieces(phase, i, lambda copy: copy.wait_send()))


def on_device(n_blk, n_frq, spectra, channel_valid):
    freq_total = spectra.shape[3] * n_frq
    rows = CB // n_frq
    scale = 1.0 / (M * math.sqrt(W * CB * freq_total))
    vmem = pl.BlockSpec(memory_space=pltpu.VMEM)
    hbm = pl.BlockSpec(memory_space=pl.ANY)
    dma = pltpu.SemaphoreType.DMA
    fine, coarse = lag_tables(freq_total)
    stacked = pl.pallas_call(
        functools.partial(kernel, n_blk, n_frq),
        out_shape=pltpu.VMEM((ROUNDS, rows, LAGS), jnp.float32),
        in_specs=[hbm, hbm, hbm, hbm, hbm, hbm],
        out_specs=vmem,
        scratch_shapes=[
            pltpu.VMEM((2, CB, W, 2 * K), jnp.bfloat16),
            pltpu.VMEM((2, K), jnp.int32),
            pltpu.VMEM((2 * M, 2 * CB), jnp.bfloat16),
            pltpu.VMEM((2 * CB, 2 * M), jnp.bfloat16),
            pltpu.VMEM((2, K, TAU), jnp.float32),
            pltpu.VMEM((2, TAU), jnp.float32),
            pltpu.VMEM((2 * K, TAU), jnp.bfloat16),
            pltpu.VMEM((CB, K), jnp.float32),
            pltpu.VMEM((2, W, 2 * CB, K), jnp.bfloat16),
            pltpu.VMEM((3, W, 2, 2 * CB, K), jnp.bfloat16),
            pltpu.VMEM((3, W, 2 * M, 2 * K), jnp.float32),
            pltpu.VMEM((2, 5, 2 * M, K), jnp.float32),
            pltpu.VMEM((2, 3, CB, TAU), jnp.bfloat16),
            pltpu.VMEM((2, 3, CB, TAU), jnp.bfloat16),
            pltpu.VMEM((2, 3, CB, TAU), jnp.bfloat16),
            pltpu.VMEM((ROUNDS, n_frq, rows, TAU), jnp.bfloat16),
            dma((5,)),
            dma((PARTS,)),
            dma((W,)),
            dma((3, W, 2)),
            dma((3, W, 2)),
            dma((2, 3)),
            dma((2, 3)),
            dma((2, 3, n_frq)),
            dma((ROUNDS, n_frq)),
            pltpu.SemaphoreType.REGULAR((3,)),
        ],
        compiler_params=pltpu.CompilerParams(collective_id=0, has_side_effects=True),
    )(
        spectra,
        channel_valid.reshape(2, K),
        jnp.asarray(forward_table()),
        jnp.asarray(inverse_table(scale)),
        jnp.asarray(fine),
        jnp.asarray(coarse),
    )
    return stacked.transpose(0, 2, 1)[None]


def solution(mesh):
    return jax.shard_map(
        functools.partial(on_device, mesh.shape["blk"], mesh.shape["frq"]),
        mesh=mesh,
        in_specs=(P(None, "blk", None, "frq"), P("blk")),
        out_specs=P("blk", None, None, "frq"),
        check_vma=False,
    )
```

```python
import functools
import math

import jax
import jax.numpy as jnp
import ml_dtypes
import numpy as np
from jax import lax
from jax.experimental import pallas as pl
from jax.experimental.pallas import tpu as pltpu
from jax.sharding import PartitionSpec as P

LAGS = 201
ROUNDS = 4
CB = 256
W = 4
M = 384
K = 128
TAU = 256
PARTS = 2
PART = CB // PARTS
EARLY = 1
LATER = 2
MESH = pl.DeviceIdType.MESH


def forward_table():
    angle = 2.0 * np.pi / M * (np.outer(np.arange(M), np.arange(CB)) % M)
    cos, sin = np.cos(angle), np.sin(angle)
    table = np.block([[cos, sin], [-sin, cos]])
    table = table.reshape(2 * M, 2, PARTS, PART).transpose(0, 2, 1, 3).reshape(2 * M, 2 * CB)
    return table.astype(ml_dtypes.bfloat16)


def inverse_table(scale):
    angle = 2.0 * np.pi / M * (np.outer(np.arange(CB) - CB // 2, np.arange(M)) % M)
    cos, sin = scale * np.cos(angle), scale * np.sin(angle)
    return np.block([[cos, -sin], [sin, cos]]).astype(ml_dtypes.bfloat16)


def lag_tables(freq_total):
    lag = np.arange(TAU) - (LAGS - 1) // 2
    keep = np.arange(TAU) < LAGS

    def waves(freq):
        angle = np.pi / freq_total * (np.outer(freq, lag) % (2 * freq_total))
        return np.stack([np.where(keep, np.cos(angle), 0.0), np.where(keep, np.sin(angle), 0.0)])

    fine = waves(np.arange(K)).astype(np.float32)
    coarse = waves(np.arange(0, freq_total, K)).transpose(1, 0, 2).astype(np.float32)
    return fine, coarse


C, D, B, E, A, F = (0, 0), (0, 1), (1, 0), (1, 1), (2, 0), (2, 1)
PHASE_PAIRS = (
    ((C, B), (E, B), (D, C), (D, B), (E, C)),
    (None, (E, A), (D, A), (F, B)),
)


def kernel(
    n_blk, n_frq, raw_hbm, valid_hbm, fwd_hbm, inv_hbm, fine_hbm, coarse_hbm, out_ref,
    raw, valid, fwd, inv, fine, coarse, lag, column, mine, near, hats, acc, part_out, part_in, piece_out, piece_in,
    load_sem, raw_sem, local_sem, send_sem, recv_sem, part_send, part_recv, piece_send, piece_recv, ready,
):
    blk = lax.axis_index("blk")
    frq = lax.axis_index("frq")
    chips = n_blk // 2
    rows = CB // n_frq
    chip, core = blk // 2, blk % 2
    right = (chip + 1) % chips
    left = (chip + chips - 1) % chips
    partner = (chip * 2 + 1 - core, frq)
    has_left, has_right = chip > 0, chip < chips - 1

    def raw_load(part):
        channels = pl.ds(part * PART, PART)
        return pltpu.make_async_copy(raw_hbm.at[:, channels], raw.at[:, channels], raw_sem.at[part])

    loads = [
        pltpu.make_async_copy(fwd_hbm, fwd, load_sem.at[0]),
        pltpu.make_async_copy(inv_hbm, inv, load_sem.at[1]),
        pltpu.make_async_copy(fine_hbm, fine, load_sem.at[2]),
        pltpu.make_async_copy(coarse_hbm.at[frq * 2 + core], coarse, load_sem.at[3]),
    ]
    valid_load = pltpu.make_async_copy(valid_hbm, valid, load_sem.at[4])
    valid_load.start()
    for part in range(PARTS):
        raw_load(part).start()

    barrier = pltpu.get_barrier_semaphore()
    side = n_frq // 2
    next_x, last_x = frq // side * side + (frq + 1) % side, frq // side * side + (frq + side - 1) % side
    across = (frq + side) % n_frq
    peers = [partner, (blk, next_x), (blk, last_x), (blk, across)]

    def greet(devices):
        for device in devices:
            pl.semaphore_signal(barrier, inc=1, device_id=device, device_id_type=MESH)

    greet(peers)
    pl.when(has_left)(lambda: greet([(left * 2 + c, frq) for c in range(2)]))
    pl.when(has_right)(lambda: greet([(right * 2 + c, frq) for c in range(2)]))

    valid_load.wait()
    here = lax.broadcasted_iota(jnp.int32, (K, K), 0) == lax.broadcasted_iota(jnp.int32, (K, K), 1)
    for part in range(CB // K):
        row = valid[part : part + 1, :].astype(jnp.float32)
        spread = jnp.where(here, jnp.broadcast_to(row, (K, K)), 0.0)
        total = jnp.sum(spread, axis=1, keepdims=True)
        column[part * K : (part + 1) * K] = jnp.broadcast_to(total, (K, K))

    def whiten(part, t, carry):
        channels = pl.ds(pl.multiple_of(part * PART + t * 16, 16), 16)
        real = pl.ds(pl.multiple_of(2 * part * PART + t * 16, 16), 16)
        imag = pl.ds(pl.multiple_of((2 * part + 1) * PART + t * 16, 16), 16)
        keep = column[channels]
        for half in range(2):
            lanes = slice(half * K, (half + 1) * K)
            both = [jnp.swapaxes(raw[r, channels, :, lanes].astype(jnp.float32), 0, 1) for r in range(2)]
            values = [(both[0][w], both[1][w]) for w in range(W)]
            power = sum(re * re + im * im for re, im in values) * (1.0 / W)
            factor = keep / jnp.maximum(jnp.sqrt(power), 0.5)
            for w, (re, im) in enumerate(values):
                mine[half, w, real] = (re * factor).astype(jnp.bfloat16)
                mine[half, w, imag] = (im * factor).astype(jnp.bfloat16)
        return carry

    def local_copy(w):
        return pltpu.make_async_copy(mine.at[core, w], near.at[0, w, core], local_sem.at[w])

    def partner_copy(w):
        return pltpu.make_async_remote_copy(
            src_ref=mine.at[1 - core, w],
            dst_ref=near.at[0, w, core],
            send_sem=send_sem.at[0, w, 0],
            recv_sem=recv_sem.at[0, w, core],
            device_id=partner,
            device_id_type=MESH,
        )

    def chip_copy(phase, w, half):
        rightward = core == (1 if phase == 1 else 0)
        side = 1 - core if phase == 1 else core
        return pltpu.make_async_remote_copy(
            src_ref=mine.at[half, w],
            dst_ref=near.at[phase, w, side],
            send_sem=send_sem.at[phase, w, half],
            recv_sem=recv_sem.at[phase, w, side],
            device_id=(jnp.where(rightward, right, left) * 2 + half, frq),
            device_id_type=MESH,
        )

    def sends(phase):
        rightward = core == (1 if phase == 1 else 0)
        return (rightward & has_right) | (~rightward & has_left)

    def first_chunk(half, part):
        chunk = pl.ds(2 * part * PART, 2 * PART)
        return pltpu.make_async_remote_copy(
            src_ref=mine.at[half, 0, chunk],
            dst_ref=near.at[1, 0, 1 - core, chunk],
            send_sem=send_sem.at[1, 0, half],
            recv_sem=recv_sem.at[1, 0, 1 - core],
            device_id=(jnp.where(core == 1, right, left) * 2 + half, frq),
            device_id_type=MESH,
        )

    for part in range(PARTS):
        raw_load(part).wait()
        lax.fori_loop(0, PART // 16, functools.partial(whiten, part), 0, unroll=2)
        if part == 0:
            pl.semaphore_wait(
                barrier, len(peers) + jnp.where(has_left, 2, 0) + jnp.where(has_right, 2, 0)
            )
        @pl.when(sends(1))
        def _():
            for half in range(2):
                first_chunk(half, part).start()

        if part == 0:
            for copy in loads:
                copy.start()
    @pl.when(sends(1))
    def _():
        for w in range(1, W):
            for half in range(2):
                chip_copy(1, w, half).start()

    for w in range(W):
        partner_copy(w).start()
        local_copy(w).start()

    for step, target in enumerate([(blk, last_x), (blk, across)]):
        pl.semaphore_signal(ready.at[step], inc=1, device_id=target, device_id_type=MESH)
        pl.semaphore_wait(ready.at[step], 1)

    @pl.when(has_left)
    def _():
        pl.semaphore_signal(ready.at[2], inc=1, device_id=(left * 2 + core, frq), device_id_type=MESH)

    @pl.when(has_right)
    def _():
        pl.semaphore_wait(ready.at[2], 1)

    acc[...] = jnp.zeros_like(acc)
    for copy in loads:
        copy.wait()
    fine_cos, fine_sin = fine[0], fine[1]
    coarse_cos, coarse_sin = coarse[0:1], coarse[1:2]
    lag[:K] = (fine_cos * coarse_cos - fine_sin * coarse_sin).astype(jnp.bfloat16)
    lag[K:] = (-(fine_sin * coarse_cos + fine_cos * coarse_sin)).astype(jnp.bfloat16)

    def wait_landed(slot, w, c):
        pltpu.make_async_copy(near.at[slot, w, c], near.at[slot, w, c], recv_sem.at[slot, w, c]).wait()

    def wait_sides(slot, w):
        pl.when(has_left)(lambda: wait_landed(slot, w, 0))
        pl.when(has_right)(lambda: wait_landed(slot, w, 1))

    def hat(slot, w):
        data = jnp.concatenate([near[slot, w, 0], near[slot, w, 1]], axis=1)
        hats[slot, w] = jnp.dot(fwd[...], data, preferred_element_type=jnp.float32)

    def cross(phase, w):
        pairs = PHASE_PAIRS[phase - 1]
        used = sorted({block for pair in pairs if pair for block in pair})

        def tile(t, carry):
            re = pl.ds(pl.multiple_of(t * 8, 8), 8)
            im = pl.ds(pl.multiple_of(M + t * 8, 8), 8)
            value = {}
            for slot, c in used:
                lanes = slice(c * K, (c + 1) * K)
                value[slot, c] = (hats[slot, w, re, lanes], hats[slot, w, im, lanes])
            for index, pair in enumerate(pairs):
                if pair is None:
                    continue
                (ar, ai), (br, bi) = value[pair[0]], value[pair[1]]
                acc[phase - 1, index, re] += ar * br + ai * bi
                acc[phase - 1, index, im] += ai * br - ar * bi
            return carry

        lax.fori_loop(0, M // 8, tile, 0, unroll=16)

    def stacked_pairs(phase, index, count):
        both = jnp.concatenate([acc[phase - 1, index + c] for c in range(count)], axis=1)
        stack = jnp.dot(inv[...], both.astype(jnp.bfloat16), preferred_element_type=jnp.float32)
        stack = stack.astype(jnp.bfloat16)
        for c in reversed(range(count)):
            lanes = slice(c * K, (c + 1) * K)
            yield c, jnp.concatenate([stack[:CB, lanes], stack[CB:, lanes]], axis=1)

    def correlation(pair):
        return jnp.dot(pair, lag[...], preferred_element_type=jnp.float32)

    def part_copy(phase, i):
        return pltpu.make_async_remote_copy(
            src_ref=part_out.at[phase - 1, i],
            dst_ref=part_in.at[phase - 1, i],
            send_sem=part_send.at[phase - 1, i],
            recv_sem=part_recv.at[phase - 1, i],
            device_id=partner,
            device_id_type=MESH,
        )

    def place(phase, i):
        if phase == 1:
            return ((0, 0), (2 - core, 1 - core), (1, 1))[i]
        return (1 + core, 0) if i == 0 else (3, 1)

    order = [half_off * side + off_x for half_off in (1, 0) for off_x in (2, 1, 3, 0)][:-1]

    def piece_rows(other):
        return pl.ds(pl.multiple_of(other * rows, rows), rows)

    def piece_copy(phase, i, off):
        j, shift = place(phase, i)
        half_off, off_x = divmod(off, side)
        other = ((frq // side + half_off) % 2) * side + (frq + off_x) % side
        return pltpu.make_async_remote_copy(
            src_ref=piece_out.at[phase - 1, i, piece_rows(other)],
            dst_ref=piece_in.at[j, frq],
            send_sem=piece_send.at[phase - 1, i, off],
            recv_sem=piece_recv.at[j, frq],
            device_id=((chip + shift) % chips * 2 + core, other),
            device_id_type=MESH,
        )

    def own_copy(phase, i):
        j, _ = place(phase, i)
        return pltpu.make_async_copy(
            piece_out.at[phase - 1, i, piece_rows(frq)], piece_in.at[j, frq], piece_recv.at[j, frq]
        )

    def only(which):
        def run(body):
            if which is None:
                body()
            else:
                pl.when(core == which)(body)

        return run

    def reducer(phase, i):
        return {(1, 2): 0, (2, 0): 1}.get((phase, i))

    def other_core(which):
        return None if which is None else 1 - which

    def pieces(phase, i, act):
        def away():
            for off in order + [0]:
                act(piece_copy(phase, i, off))

        def here():
            for off in order:
                act(piece_copy(phase, i, off))

        if i == 0:
            here()
        elif (phase, i) != (1, 1):
            pl.when(has_right)(away)
        else:
            pl.when((core == 0) & has_right)(away)
            pl.when(core == 1)(here)

    def start_pieces(phase, i):
        pieces(phase, i, lambda copy: copy.start())
        if i == 0:
            own_copy(phase, i).start()
        elif (phase, i) == (1, 1):
            pl.when(core == 1)(lambda: own_copy(1, 1).start())

    def give_part(phase, i, pair):
        @only(other_core(reducer(phase, i)))
        def _():
            part_out[phase - 1, i] = correlation(pair).astype(jnp.bfloat16)
            part_copy(phase, i).start()

    def give_pieces(phase, i, pair):
        @only(reducer(phase, i))
        def _():
            value = correlation(pair)
            part_copy(phase, i).wait_recv()
            both = value + part_in[phase - 1, i].astype(jnp.float32)
            piece_out[phase - 1, i] = both.astype(jnp.bfloat16)
            start_pieces(phase, i)

    def scatter(phase):
        if phase == 1:
            @only(1)
            def _():
                for _, pair in stacked_pairs(1, 4, 1):
                    part_out[0, 2] = correlation(pair).astype(jnp.bfloat16)
                part_copy(1, 2).start()

        for i, pair in stacked_pairs(phase, (1 - core) * 2, 2):
            give_part(phase, i, pair)
        for i, pair in stacked_pairs(phase, core * 2, 2):
            give_pieces(phase, i, pair)
        if phase == 1:
            @only(0)
            def _():
                for _, pair in stacked_pairs(1, 4, 1):
                    value = correlation(pair)
                part_copy(1, 2).wait_recv()
                both = value + part_in[0, 2].astype(jnp.float32)
                piece_out[0, 2] = both.astype(jnp.bfloat16)
                start_pieces(1, 2)

    def first(w, carry):
        local_copy(w).wait()
        wait_landed(0, w, 1 - core)
        hat(0, w)
        wait_sides(1, w)
        hat(1, w)
        cross(1, w)
        return carry

    def send_second(windows):
        @pl.when(sends(2))
        def _():
            for w in windows:
                for half in range(2):
                    chip_copy(2, w, half).start()

    lax.fori_loop(0, EARLY, first, 0)
    send_second(range(1))
    lax.fori_loop(EARLY, LATER, first, 0)
    send_second(range(1, W))
    lax.fori_loop(LATER, W, first, 0)
    scatter(1)

    def second(w, carry):
        wait_sides(2, w)
        hat(2, w)
        cross(2, w)
        return carry

    lax.fori_loop(0, W, second, 0)
    scatter(2)

    for j in range(ROUNDS):
        total = jnp.zeros((rows, TAU), jnp.float32)
        come = True if j == 0 else has_left if j == 3 else (core == 1) | has_left

        @pl.when(come)
        def _():
            for f in range(n_frq):
                pltpu.make_async_copy(piece_in.at[j, f], piece_in.at[j, f], piece_recv.at[j, f]).wait()

        for f in range(n_frq):
            total += piece_in[j, f].astype(jnp.float32)
        total = jnp.where(blk > j, total, 0.0)
        out_ref[j] = total[:, :LAGS]

    for w in range(W):
        partner_copy(w).wait_send()
    for phase in (1, 2):
        @pl.when(sends(phase))
        def _():
            for w in range(W):
                for half in range(2):
                    chip_copy(phase, w, half).wait_send()

    for phase, i in ((1, 0), (1, 1), (1, 2), (2, 0), (2, 1)):
        @only(other_core(reducer(phase, i)))
        def _():
            part_copy(phase, i).wait_send()

        only(reducer(phase, i))(lambda: pieces(phase, i, lambda copy: copy.wait_send()))


def on_device(n_blk, n_frq, spectra, channel_valid):
    freq_total = spectra.shape[3] * n_frq
    rows = CB // n_frq
    scale = 1.0 / (M * math.sqrt(W * CB * freq_total))
    vmem = pl.BlockSpec(memory_space=pltpu.VMEM)
    hbm = pl.BlockSpec(memory_space=pl.ANY)
    dma = pltpu.SemaphoreType.DMA
    fine, coarse = lag_tables(freq_total)
    stacked = pl.pallas_call(
        functools.partial(kernel, n_blk, n_frq),
        out_shape=pltpu.VMEM((ROUNDS, rows, LAGS), jnp.float32),
        in_specs=[hbm, hbm, hbm, hbm, hbm, hbm],
        out_specs=vmem,
        scratch_shapes=[
            pltpu.VMEM((2, CB, W, 2 * K), jnp.bfloat16),
            pltpu.VMEM((2, K), jnp.int32),
            pltpu.VMEM((2 * M, 2 * CB), jnp.bfloat16),
            pltpu.VMEM((2 * CB, 2 * M), jnp.bfloat16),
            pltpu.VMEM((2, K, TAU), jnp.float32),
            pltpu.VMEM((2, TAU), jnp.float32),
            pltpu.VMEM((2 * K, TAU), jnp.bfloat16),
            pltpu.VMEM((CB, K), jnp.float32),
            pltpu.VMEM((2, W, 2 * CB, K), jnp.bfloat16),
            pltpu.VMEM((3, W, 2, 2 * CB, K), jnp.bfloat16),
            pltpu.VMEM((3, W, 2 * M, 2 * K), jnp.float32),
            pltpu.VMEM((2, 5, 2 * M, K), jnp.float32),
            pltpu.VMEM((2, 3, CB, TAU), jnp.bfloat16),
            pltpu.VMEM((2, 3, CB, TAU), jnp.bfloat16),
            pltpu.VMEM((2, 3, CB, TAU), jnp.bfloat16),
            pltpu.VMEM((ROUNDS, n_frq, rows, TAU), jnp.bfloat16),
            dma((5,)),
            dma((PARTS,)),
            dma((W,)),
            dma((3, W, 2)),
            dma((3, W, 2)),
            dma((2, 3)),
            dma((2, 3)),
            dma((2, 3, n_frq)),
            dma((ROUNDS, n_frq)),
            pltpu.SemaphoreType.REGULAR((3,)),
        ],
        compiler_params=pltpu.CompilerParams(collective_id=0, has_side_effects=True),
    )(
        spectra,
        channel_valid.reshape(2, K),
        jnp.asarray(forward_table()),
        jnp.asarray(inverse_table(scale)),
        jnp.asarray(fine),
        jnp.asarray(coarse),
    )
    return stacked.transpose(0, 2, 1)[None]


def solution(mesh):
    return jax.shard_map(
        functools.partial(on_device, mesh.shape["blk"], mesh.shape["frq"]),
        mesh=mesh,
        in_specs=(P(None, "blk", None, "frq"), P("blk")),
        out_specs=P("blk", None, None, "frq"),
        check_vma=False,
    )
```

```python
import functools
import math

import jax
import jax.numpy as jnp
import ml_dtypes
import numpy as np
from jax import lax
from jax.experimental import pallas as pl
from jax.experimental.pallas import tpu as pltpu
from jax.sharding import PartitionSpec as P

LAGS = 201
ROUNDS = 4
CB = 256
W = 4
M = 384
K = 128
TAU = 256
PARTS = 2
PART = CB // PARTS
EARLY = 1
LATER = 3
MESH = pl.DeviceIdType.MESH


def forward_table():
    angle = 2.0 * np.pi / M * (np.outer(np.arange(M), np.arange(CB)) % M)
    cos, sin = np.cos(angle), np.sin(angle)
    table = np.block([[cos, sin], [-sin, cos]])
    table = table.reshape(2 * M, 2, PARTS, PART).transpose(0, 2, 1, 3).reshape(2 * M, 2 * CB)
    return table.astype(ml_dtypes.bfloat16)


def inverse_table(scale):
    angle = 2.0 * np.pi / M * (np.outer(np.arange(CB) - CB // 2, np.arange(M)) % M)
    cos, sin = scale * np.cos(angle), scale * np.sin(angle)
    return np.block([[cos, -sin], [sin, cos]]).astype(ml_dtypes.bfloat16)


def lag_tables(freq_total):
    lag = np.arange(TAU) - (LAGS - 1) // 2
    keep = np.arange(TAU) < LAGS

    def waves(freq):
        angle = np.pi / freq_total * (np.outer(freq, lag) % (2 * freq_total))
        return np.stack([np.where(keep, np.cos(angle), 0.0), np.where(keep, np.sin(angle), 0.0)])

    fine = waves(np.arange(K)).astype(np.float32)
    coarse = waves(np.arange(0, freq_total, K)).transpose(1, 0, 2).astype(np.float32)
    return fine, coarse


C, D, B, E, A, F = (0, 0), (0, 1), (1, 0), (1, 1), (2, 0), (2, 1)
PHASE_PAIRS = (
    ((C, B), (E, B), (D, C), (D, B), (E, C)),
    (None, (E, A), (D, A), (F, B)),
)


def kernel(
    n_blk, n_frq, raw_hbm, valid_hbm, fwd_hbm, inv_hbm, fine_hbm, coarse_hbm, out_ref,
    raw, valid, fwd, inv, fine, coarse, lag, column, mine, near, hats, acc, part_out, part_in, piece_out, piece_in,
    load_sem, raw_sem, local_sem, send_sem, recv_sem, part_send, part_recv, piece_send, piece_recv, ready,
):
    blk = lax.axis_index("blk")
    frq = lax.axis_index("frq")
    chips = n_blk // 2
    rows = CB // n_frq
    chip, core = blk // 2, blk % 2
    right = (chip + 1) % chips
    left = (chip + chips - 1) % chips
    partner = (chip * 2 + 1 - core, frq)
    has_left, has_right = chip > 0, chip < chips - 1

    def raw_load(part):
        channels = pl.ds(part * PART, PART)
        return pltpu.make_async_copy(raw_hbm.at[:, channels], raw.at[:, channels], raw_sem.at[part])

    loads = [
        pltpu.make_async_copy(fwd_hbm, fwd, load_sem.at[0]),
        pltpu.make_async_copy(inv_hbm, inv, load_sem.at[1]),
        pltpu.make_async_copy(fine_hbm, fine, load_sem.at[2]),
        pltpu.make_async_copy(coarse_hbm.at[frq * 2 + core], coarse, load_sem.at[3]),
    ]
    valid_load = pltpu.make_async_copy(valid_hbm, valid, load_sem.at[4])
    valid_load.start()
    for part in range(PARTS):
        raw_load(part).start()

    barrier = pltpu.get_barrier_semaphore()
    side = n_frq // 2
    next_x, last_x = frq // side * side + (frq + 1) % side, frq // side * side + (frq + side - 1) % side
    across = (frq + side) % n_frq
    peers = [partner, (blk, next_x), (blk, last_x), (blk, across)]

    def greet(devices):
        for device in devices:
            pl.semaphore_signal(barrier, inc=1, device_id=device, device_id_type=MESH)

    greet(peers)
    pl.when(has_left)(lambda: greet([(left * 2 + c, frq) for c in range(2)]))
    pl.when(has_right)(lambda: greet([(right * 2 + c, frq) for c in range(2)]))

    valid_load.wait()
    here = lax.broadcasted_iota(jnp.int32, (K, K), 0) == lax.broadcasted_iota(jnp.int32, (K, K), 1)
    for part in range(CB // K):
        row = valid[part : part + 1, :].astype(jnp.float32)
        spread = jnp.where(here, jnp.broadcast_to(row, (K, K)), 0.0)
        total = jnp.sum(spread, axis=1, keepdims=True)
        column[part * K : (part + 1) * K] = jnp.broadcast_to(total, (K, K))

    def whiten(part, t, carry):
        channels = pl.ds(pl.multiple_of(part * PART + t * 16, 16), 16)
        real = pl.ds(pl.multiple_of(2 * part * PART + t * 16, 16), 16)
        imag = pl.ds(pl.multiple_of((2 * part + 1) * PART + t * 16, 16), 16)
        keep = column[channels]
        for half in range(2):
            lanes = slice(half * K, (half + 1) * K)
            both = [jnp.swapaxes(raw[r, channels, :, lanes].astype(jnp.float32), 0, 1) for r in range(2)]
            values = [(both[0][w], both[1][w]) for w in range(W)]
            power = sum(re * re + im * im for re, im in values) * (1.0 / W)
            factor = keep / jnp.maximum(jnp.sqrt(power), 0.5)
            for w, (re, im) in enumerate(values):
                mine[half, w, real] = (re * factor).astype(jnp.bfloat16)
                mine[half, w, imag] = (im * factor).astype(jnp.bfloat16)
        return carry

    def local_copy(w):
        return pltpu.make_async_copy(mine.at[core, w], near.at[0, w, core], local_sem.at[w])

    def partner_copy(w):
        return pltpu.make_async_remote_copy(
            src_ref=mine.at[1 - core, w],
            dst_ref=near.at[0, w, core],
            send_sem=send_sem.at[0, w, 0],
            recv_sem=recv_sem.at[0, w, core],
            device_id=partner,
            device_id_type=MESH,
        )

    def chip_copy(phase, w, half):
        rightward = core == (1 if phase == 1 else 0)
        side = 1 - core if phase == 1 else core
        return pltpu.make_async_remote_copy(
            src_ref=mine.at[half, w],
            dst_ref=near.at[phase, w, side],
            send_sem=send_sem.at[phase, w, half],
            recv_sem=recv_sem.at[phase, w, side],
            device_id=(jnp.where(rightward, right, left) * 2 + half, frq),
            device_id_type=MESH,
        )

    def sends(phase):
        rightward = core == (1 if phase == 1 else 0)
        return (rightward & has_right) | (~rightward & has_left)

    def first_chunk(half, part):
        chunk = pl.ds(2 * part * PART, 2 * PART)
        return pltpu.make_async_remote_copy(
            src_ref=mine.at[half, 0, chunk],
            dst_ref=near.at[1, 0, 1 - core, chunk],
            send_sem=send_sem.at[1, 0, half],
            recv_sem=recv_sem.at[1, 0, 1 - core],
            device_id=(jnp.where(core == 1, right, left) * 2 + half, frq),
            device_id_type=MESH,
        )

    for part in range(PARTS):
        raw_load(part).wait()
        lax.fori_loop(0, PART // 16, functools.partial(whiten, part), 0, unroll=2)
        if part == 0:
            pl.semaphore_wait(
                barrier, len(peers) + jnp.where(has_left, 2, 0) + jnp.where(has_right, 2, 0)
            )
        @pl.when(sends(1))
        def _():
            for half in range(2):
                first_chunk(half, part).start()

        if part == 0:
            for copy in loads:
                copy.start()
    @pl.when(sends(1))
    def _():
        for w in range(1, W):
            for half in range(2):
                chip_copy(1, w, half).start()

    for w in range(W):
        partner_copy(w).start()
        local_copy(w).start()

    for step, target in enumerate([(blk, last_x), (blk, across)]):
        pl.semaphore_signal(ready.at[step], inc=1, device_id=target, device_id_type=MESH)
        pl.semaphore_wait(ready.at[step], 1)

    @pl.when(has_left)
    def _():
        pl.semaphore_signal(ready.at[2], inc=1, device_id=(left * 2 + core, frq), device_id_type=MESH)

    @pl.when(has_right)
    def _():
        pl.semaphore_wait(ready.at[2], 1)

    acc[...] = jnp.zeros_like(acc)
    for copy in loads:
        copy.wait()
    fine_cos, fine_sin = fine[0], fine[1]
    coarse_cos, coarse_sin = coarse[0:1], coarse[1:2]
    lag[:K] = (fine_cos * coarse_cos - fine_sin * coarse_sin).astype(jnp.bfloat16)
    lag[K:] = (-(fine_sin * coarse_cos + fine_cos * coarse_sin)).astype(jnp.bfloat16)

    def wait_landed(slot, w, c):
        pltpu.make_async_copy(near.at[slot, w, c], near.at[slot, w, c], recv_sem.at[slot, w, c]).wait()

    def wait_sides(slot, w):
        pl.when(has_left)(lambda: wait_landed(slot, w, 0))
        pl.when(has_right)(lambda: wait_landed(slot, w, 1))

    def hat(slot, w):
        data = jnp.concatenate([near[slot, w, 0], near[slot, w, 1]], axis=1)
        hats[slot, w] = jnp.dot(fwd[...], data, preferred_element_type=jnp.float32)

    def cross(phase, w):
        pairs = PHASE_PAIRS[phase - 1]
        used = sorted({block for pair in pairs if pair for block in pair})

        def tile(t, carry):
            re = pl.ds(pl.multiple_of(t * 8, 8), 8)
            im = pl.ds(pl.multiple_of(M + t * 8, 8), 8)
            value = {}
            for slot, c in used:
                lanes = slice(c * K, (c + 1) * K)
                value[slot, c] = (hats[slot, w, re, lanes], hats[slot, w, im, lanes])
            for index, pair in enumerate(pairs):
                if pair is None:
                    continue
                (ar, ai), (br, bi) = value[pair[0]], value[pair[1]]
                acc[phase - 1, index, re] += ar * br + ai * bi
                acc[phase - 1, index, im] += ai * br - ar * bi
            return carry

        lax.fori_loop(0, M // 8, tile, 0, unroll=16)

    def stacked_pairs(phase, index, count):
        both = jnp.concatenate([acc[phase - 1, index + c] for c in range(count)], axis=1)
        stack = jnp.dot(inv[...], both.astype(jnp.bfloat16), preferred_element_type=jnp.float32)
        stack = stack.astype(jnp.bfloat16)
        for c in reversed(range(count)):
            lanes = slice(c * K, (c + 1) * K)
            yield c, jnp.concatenate([stack[:CB, lanes], stack[CB:, lanes]], axis=1)

    def correlation(pair):
        return jnp.dot(pair, lag[...], preferred_element_type=jnp.float32)

    def part_copy(phase, i):
        return pltpu.make_async_remote_copy(
            src_ref=part_out.at[phase - 1, i],
            dst_ref=part_in.at[phase - 1, i],
            send_sem=part_send.at[phase - 1, i],
            recv_sem=part_recv.at[phase - 1, i],
            device_id=partner,
            device_id_type=MESH,
        )

    def place(phase, i):
        if phase == 1:
            return ((0, 0), (2 - core, 1 - core), (1, 1))[i]
        return (1 + core, 0) if i == 0 else (3, 1)

    order = [half_off * side + off_x for half_off in (1, 0) for off_x in (2, 1, 3, 0)][:-1]

    def piece_rows(other):
        return pl.ds(pl.multiple_of(other * rows, rows), rows)

    def piece_copy(phase, i, off):
        j, shift = place(phase, i)
        half_off, off_x = divmod(off, side)
        other = ((frq // side + half_off) % 2) * side + (frq + off_x) % side
        return pltpu.make_async_remote_copy(
            src_ref=piece_out.at[phase - 1, i, piece_rows(other)],
            dst_ref=piece_in.at[j, frq],
            send_sem=piece_send.at[phase - 1, i, off],
            recv_sem=piece_recv.at[j, frq],
            device_id=((chip + shift) % chips * 2 + core, other),
            device_id_type=MESH,
        )

    def own_copy(phase, i):
        j, _ = place(phase, i)
        return pltpu.make_async_copy(
            piece_out.at[phase - 1, i, piece_rows(frq)], piece_in.at[j, frq], piece_recv.at[j, frq]
        )

    def only(which):
        def run(body):
            if which is None:
                body()
            else:
                pl.when(core == which)(body)

        return run

    def reducer(phase, i):
        return {(1, 2): 0, (2, 0): 1}.get((phase, i))

    def other_core(which):
        return None if which is None else 1 - which

    def pieces(phase, i, act):
        def away():
            for off in order + [0]:
                act(piece_copy(phase, i, off))

        def here():
            for off in order:
                act(piece_copy(phase, i, off))

        if i == 0:
            here()
        elif (phase, i) != (1, 1):
            pl.when(has_right)(away)
        else:
            pl.when((core == 0) & has_right)(away)
            pl.when(core == 1)(here)

    def start_pieces(phase, i):
        pieces(phase, i, lambda copy: copy.start())
        if i == 0:
            own_copy(phase, i).start()
        elif (phase, i) == (1, 1):
            pl.when(core == 1)(lambda: own_copy(1, 1).start())

    def give_part(phase, i, pair):
        @only(other_core(reducer(phase, i)))
        def _():
            part_out[phase - 1, i] = correlation(pair).astype(jnp.bfloat16)
            part_copy(phase, i).start()

    def give_pieces(phase, i, pair):
        @only(reducer(phase, i))
        def _():
            value = correlation(pair)
            part_copy(phase, i).wait_recv()
            both = value + part_in[phase - 1, i].astype(jnp.float32)
            piece_out[phase - 1, i] = both.astype(jnp.bfloat16)
            start_pieces(phase, i)

    def scatter(phase):
        if phase == 1:
            @only(1)
            def _():
                for _, pair in stacked_pairs(1, 4, 1):
                    part_out[0, 2] = correlation(pair).astype(jnp.bfloat16)
                part_copy(1, 2).start()

        for i, pair in stacked_pairs(phase, (1 - core) * 2, 2):
            give_part(phase, i, pair)
        for i, pair in stacked_pairs(phase, core * 2, 2):
            give_pieces(phase, i, pair)
        if phase == 1:
            @only(0)
            def _():
                for _, pair in stacked_pairs(1, 4, 1):
                    value = correlation(pair)
                part_copy(1, 2).wait_recv()
                both = value + part_in[0, 2].astype(jnp.float32)
                piece_out[0, 2] = both.astype(jnp.bfloat16)
                start_pieces(1, 2)

    def first(w, carry):
        local_copy(w).wait()
        wait_landed(0, w, 1 - core)
        hat(0, w)
        wait_sides(1, w)
        hat(1, w)
        cross(1, w)
        return carry

    def send_second(windows):
        @pl.when(sends(2))
        def _():
            for w in windows:
                for half in range(2):
                    chip_copy(2, w, half).start()

    lax.fori_loop(0, EARLY, first, 0)
    send_second(range(1))
    lax.fori_loop(EARLY, LATER, first, 0)
    send_second(range(1, W))
    lax.fori_loop(LATER, W, first, 0)
    scatter(1)

    def second(w, carry):
        wait_sides(2, w)
        hat(2, w)
        cross(2, w)
        return carry

    lax.fori_loop(0, W, second, 0)
    scatter(2)

    for j in range(ROUNDS):
        total = jnp.zeros((rows, TAU), jnp.float32)
        come = True if j == 0 else has_left if j == 3 else (core == 1) | has_left

        @pl.when(come)
        def _():
            for f in range(n_frq):
                pltpu.make_async_copy(piece_in.at[j, f], piece_in.at[j, f], piece_recv.at[j, f]).wait()

        for f in range(n_frq):
            total += piece_in[j, f].astype(jnp.float32)
        total = jnp.where(blk > j, total, 0.0)
        out_ref[j] = total[:, :LAGS]

    for w in range(W):
        partner_copy(w).wait_send()
    for phase in (1, 2):
        @pl.when(sends(phase))
        def _():
            for w in range(W):
                for half in range(2):
                    chip_copy(phase, w, half).wait_send()

    for phase, i in ((1, 0), (1, 1), (1, 2), (2, 0), (2, 1)):
        @only(other_core(reducer(phase, i)))
        def _():
            part_copy(phase, i).wait_send()

        only(reducer(phase, i))(lambda: pieces(phase, i, lambda copy: copy.wait_send()))


def on_device(n_blk, n_frq, spectra, channel_valid):
    freq_total = spectra.shape[3] * n_frq
    rows = CB // n_frq
    scale = 1.0 / (M * math.sqrt(W * CB * freq_total))
    vmem = pl.BlockSpec(memory_space=pltpu.VMEM)
    hbm = pl.BlockSpec(memory_space=pl.ANY)
    dma = pltpu.SemaphoreType.DMA
    fine, coarse = lag_tables(freq_total)
    stacked = pl.pallas_call(
        functools.partial(kernel, n_blk, n_frq),
        out_shape=pltpu.VMEM((ROUNDS, rows, LAGS), jnp.float32),
        in_specs=[hbm, hbm, hbm, hbm, hbm, hbm],
        out_specs=vmem,
        scratch_shapes=[
            pltpu.VMEM((2, CB, W, 2 * K), jnp.bfloat16),
            pltpu.VMEM((2, K), jnp.int32),
            pltpu.VMEM((2 * M, 2 * CB), jnp.bfloat16),
            pltpu.VMEM((2 * CB, 2 * M), jnp.bfloat16),
            pltpu.VMEM((2, K, TAU), jnp.float32),
            pltpu.VMEM((2, TAU), jnp.float32),
            pltpu.VMEM((2 * K, TAU), jnp.bfloat16),
            pltpu.VMEM((CB, K), jnp.float32),
            pltpu.VMEM((2, W, 2 * CB, K), jnp.bfloat16),
            pltpu.VMEM((3, W, 2, 2 * CB, K), jnp.bfloat16),
            pltpu.VMEM((3, W, 2 * M, 2 * K), jnp.float32),
            pltpu.VMEM((2, 5, 2 * M, K), jnp.float32),
            pltpu.VMEM((2, 3, CB, TAU), jnp.bfloat16),
            pltpu.VMEM((2, 3, CB, TAU), jnp.bfloat16),
            pltpu.VMEM((2, 3, CB, TAU), jnp.bfloat16),
            pltpu.VMEM((ROUNDS, n_frq, rows, TAU), jnp.bfloat16),
            dma((5,)),
            dma((PARTS,)),
            dma((W,)),
            dma((3, W, 2)),
            dma((3, W, 2)),
            dma((2, 3)),
            dma((2, 3)),
            dma((2, 3, n_frq)),
            dma((ROUNDS, n_frq)),
            pltpu.SemaphoreType.REGULAR((3,)),
        ],
        compiler_params=pltpu.CompilerParams(collective_id=0, has_side_effects=True),
    )(
        spectra,
        channel_valid.reshape(2, K),
        jnp.asarray(forward_table()),
        jnp.asarray(inverse_table(scale)),
        jnp.asarray(fine),
        jnp.asarray(coarse),
    )
    return stacked.transpose(0, 2, 1)[None]


def solution(mesh):
    return jax.shard_map(
        functools.partial(on_device, mesh.shape["blk"], mesh.shape["frq"]),
        mesh=mesh,
        in_specs=(P(None, "blk", None, "frq"), P("blk")),
        out_specs=P("blk", None, None, "frq"),
        check_vma=False,
    )
```
